32 devices in a mesh: groups: 2 (over y), latent: 4 (over z), rows: 4 (over x, core).
Axes of the slice: x: 2, y: 2, z: 4, core: 2. Of those that a mesh axis runs over, the one named last changes fastest.
Arguments:
- activations_in: bfloat16 [2, 128, 2304], P('groups', None, 'latent'), parts along dimension 0, may hold values from -6 to 6
- gate_proj: bfloat16 [2304, 4608], P('rows', 'latent'), may hold values from -0.125 to 0.125
- up_proj: bfloat16 [2304, 4608], P('rows', 'latent'), may hold values from -0.125 to 0.125
- down_proj: bfloat16 [4608, 2304], P('latent', 'rows'), may hold values from -0.09375 to 0.09375
- enc_weight: bfloat16 [4608, 65536], P(('groups', 'rows'), 'latent'), parts along dimension 0, may hold values from -6 to 6
- enc_bias: float32 [131072], P(('groups', 'latent')), parts along dimension 0, may hold values from -0.5 to 0.5
- dec_weight: bfloat16 [131072, 2304], P(('groups', 'latent'), 'rows'), parts along dimension 0, may hold values from -6 to 6
- dec_bias: float32 [4608], P(('groups', 'rows')), parts along dimension 0, may hold values from -0.5 to 0.5
Outputs:
- enc_weight_new: bfloat16 [4608, 65536], P(('groups', 'rows'), 'latent'), parts along dimension 0
- enc_bias_new: float32 [131072], P(('groups', 'latent')), parts along dimension 0
- dec_weight_new: bfloat16 [131072, 2304], P(('groups', 'latent'), 'rows'), parts along dimension 0
- dec_bias_new: float32 [4608], P(('groups', 'rows')), parts along dimension 0
The draws below stay inside these ranges and needn't reach their ends.
There are 2 independent parts, one for each index of `groups`. The reference program is written for one: setup_inputs(seed, part) draws one part's arguments, and reference() takes and returns one part's arrays. A program takes and returns all parts, laid end to end along the dimension named above; an argument that names none is the same for every part. Nothing has to cross between parts.
All inputs are finite; a program needn't handle non-finite values.
Results may differ from the reference program's by a relative error of at most 0.02.
Values may be sent and summed in bfloat16 or wider, within the bound.
A program may use at most 128 MiB of HBM per device.

```python
import jax
import jax.numpy as jnp
from jax import lax

MODEL_WIDTH = 2304
HIDDEN_UNITS = 4608
LATENTS = 65536
MINIBATCHES = 1
BATCH_TOKENS = 128
N_ROWS = 4


def level_of(rng, extent, shards, least, top_value):
    def one(dim, shards_of):
        heights = jax.random.uniform(jax.random.fold_in(jax.random.fold_in(rng, 6), dim), (shards_of,), jnp.float32, least / len(shards), top_value / len(shards))
        return jnp.repeat(jnp.exp(heights), extent[dim] // shards_of).reshape((-1,) + (1,) * (len(extent) - dim - 1))

    loudness = one(*shards[0])
    for cut in shards[1:]:
        loudness = loudness * one(*cut)
    return loudness


def noise(stream_key, extent, deviation, bound, cuts=(), dtype=jnp.bfloat16):
    result = jax.random.normal(stream_key, extent, jnp.float32) * deviation
    if len(cuts) > 0:
        result = level_of(stream_key, extent, cuts, -0.22, 0.18) * result
    return jnp.clip(result, min=-bound, max=bound).astype(dtype)


def setup_inputs(seed: int = 0, part: int = 0) -> dict:
    key_list = jax.random.split(jax.random.key(seed), 9)
    own_keys = jax.random.split(jax.random.fold_in(key_list[8], part), 9)
    return {
        "activations_in": noise(own_keys[0], (MINIBATCHES, BATCH_TOKENS, MODEL_WIDTH), 1.0, 6.0, ((2, 4),)),
        "gate_proj": noise(key_list[1], (MODEL_WIDTH, HIDDEN_UNITS), MODEL_WIDTH ** -0.5, 0.125, ((0, 4), (1, 4))),
        "up_proj": noise(key_list[2], (MODEL_WIDTH, HIDDEN_UNITS), MODEL_WIDTH ** -0.5, 0.125, ((0, 4), (1, 4))),
        "down_proj": noise(key_list[3], (HIDDEN_UNITS, MODEL_WIDTH), HIDDEN_UNITS ** -0.5, 0.09375, ((0, 4), (1, 4))),
        "enc_weight": noise(own_keys[4], (MODEL_WIDTH, LATENTS), 1.0, 6.0, ((0, 4), (1, 4))),
        "enc_bias": jnp.clip(jax.random.uniform(own_keys[5], (LATENTS,), jnp.float32, -0.5, 0.5) * level_of(own_keys[5], (LATENTS,), ((0, 4),), -0.4, 0.0), -0.5, 0.5),
        "dec_weight": noise(own_keys[6], (LATENTS, MODEL_WIDTH), 1.0, 6.0, ((0, 4), (1, 4))),
        "dec_bias": jnp.clip(jax.random.uniform(own_keys[7], (MODEL_WIDTH,), jnp.float32, -0.5, 0.5) * level_of(own_keys[7], (MODEL_WIDTH,), ((0, 4),), -0.4, 0.0), -0.5, 0.5),
    }


sparsity_cost = 0.1
sharpness = 8.0
weight_rate = 2.0
enc_bias_rate = 0.01
dec_bias_rate = 0.002


def smooth_relu(values):
    return jax.nn.softplus(sharpness * values) / sharpness


def reference(activations_in, gate_proj, up_proj, down_proj, enc_weight, enc_bias, dec_weight, dec_bias):
    flattened = activations_in.reshape(MINIBATCHES * BATCH_TOKENS, MODEL_WIDTH)
    gate_term = jnp.dot(flattened, gate_proj, preferred_element_type=jnp.float32)
    up_term = jnp.dot(flattened, up_proj, preferred_element_type=jnp.float32)
    hidden = (jax.nn.gelu(gate_term, approximate=True) * up_term).astype(jnp.bfloat16)
    features = jnp.dot(hidden, down_proj, preferred_element_type=jnp.float32).astype(jnp.bfloat16)
    features = features.reshape(MINIBATCHES, BATCH_TOKENS, MODEL_WIDTH)
    block_size = MODEL_WIDTH // N_ROWS
    enc_scale = MODEL_WIDTH ** -0.5
    dec_scale = LATENTS ** -0.5
    for batch_index in range(MINIBATCHES):
        inputs = features[batch_index]
        encoded = jnp.zeros((BATCH_TOKENS, LATENTS), jnp.float32)
        back_sum = jnp.zeros((BATCH_TOKENS, LATENTS), jnp.float32)
        for row_index in range(N_ROWS):
            lower = row_index * block_size
            term = jnp.dot(inputs[:, lower:lower + block_size], enc_weight[lower:lower + block_size],
                           preferred_element_type=jnp.float32).astype(jnp.bfloat16)
            encoded = encoded + lax.optimization_barrier(term).astype(jnp.float32)
        pre_latent = enc_scale * encoded + enc_bias
        latents = smooth_relu(pre_latent).astype(jnp.bfloat16)
        rebuilt = dec_scale * jnp.dot(latents, dec_weight, preferred_element_type=jnp.float32) + dec_bias
        residual_grad = (2.0 * (rebuilt - inputs.astype(jnp.float32))).astype(jnp.bfloat16)
        for row_index in range(N_ROWS):
            lower = row_index * block_size
            term = lax.dot_general(residual_grad[:, lower:lower + block_size], dec_weight[:, lower:lower + block_size],
                                   (((1,), (1,)), ((), ())), preferred_element_type=jnp.float32).astype(jnp.bfloat16)
            back_sum = back_sum + lax.optimization_barrier(term).astype(jnp.float32)
        latent_grad = (jax.nn.sigmoid(sharpness * pre_latent) * (dec_scale * back_sum + sparsity_cost)).astype(jnp.bfloat16)
        dec_grad = dec_scale * lax.dot_general(latents, residual_grad, (((0,), (0,)), ((), ())),
                                               preferred_element_type=jnp.float32)
        enc_grad = enc_scale * lax.dot_general(inputs, latent_grad, (((0,), (0,)), ((), ())),
                                               preferred_element_type=jnp.float32)
        enc_bias = enc_bias - enc_bias_rate * jnp.sum(latent_grad.astype(jnp.float32), axis=0)
        dec_bias = dec_bias - dec_bias_rate * jnp.sum(residual_grad.astype(jnp.float32), axis=0)
        enc_weight = (enc_weight.astype(jnp.float32) - weight_rate * enc_grad).astype(jnp.bfloat16)
        dec_weight = (dec_weight.astype(jnp.float32) - weight_rate * dec_grad).astype(jnp.bfloat16)
    return enc_weight, enc_bias, dec_weight, dec_bias
```

```python
import functools

import jax
import jax.numpy as jnp
from jax import lax
from jax.experimental import pallas as pl
from jax.experimental.pallas import tpu as pltpu
from jax.sharding import PartitionSpec as P

MODEL_WIDTH = 2304
LATENTS = 65536


sparsity_cost = 0.1
sharpness = 8.0
weight_rate = 2.0
enc_bias_rate = 0.01
dec_bias_rate = 0.002

BF16 = jnp.bfloat16
F32 = jnp.float32
CHUNKS = 8


def swap(x, axis, n, bit):
    return lax.ppermute(x, axis, [(i, i ^ bit) for i in range(n)])


def halves_scatter(x, axis, n, wire):
    me = lax.axis_index(axis)
    bit = 1
    while bit < n:
        size = x.shape[0] // 2
        mine = (me // bit) % 2
        keep = lax.dynamic_slice_in_dim(x, mine * size, size, 0)
        give = lax.dynamic_slice_in_dim(x, (1 - mine) * size, size, 0)
        got = swap(give.astype(wire), axis, n, bit)
        x = keep.astype(F32) + got.astype(F32)
        bit *= 2
    return x


def halves_gather(x, axis, n):
    me = lax.axis_index(axis)
    bit = n // 2
    while bit >= 1:
        got = swap(x, axis, n, bit)
        first = ((me // bit) % 2) == 0
        x = jnp.concatenate([jnp.where(first, x, got), jnp.where(first, got, x)], axis=0)
        bit //= 2
    return x


def direct_scatter(x, axis, n, wire):
    me = lax.axis_index(axis)
    size = x.shape[0] // n
    total = lax.dynamic_slice_in_dim(x, me * size, size, 0)
    gots = []
    for shift in range(1, n):
        to = lax.rem(me + shift, n)
        give = lax.dynamic_slice_in_dim(x, to * size, size, 0).astype(wire)
        gots.append(lax.ppermute(give, axis, [(i, (i + shift) % n) for i in range(n)]))
    for got in gots:
        total = total + got.astype(F32)
    return total


def direct_gather(x, axis, n):
    me = lax.axis_index(axis)
    size = x.shape[0]
    out = jnp.zeros((size * n,) + x.shape[1:], x.dtype)
    parts = [(me, x)]
    for shift in range(1, n):
        got = lax.ppermute(x, axis, [(i, (i + shift) % n) for i in range(n)])
        parts.append((lax.rem(me - shift + n, n), got))
    for at, part in parts:
        out = lax.dynamic_update_slice_in_dim(out, part, at * size, 0)
    return out


def update_kernel(rate, has_buf, left_ref, right_ref, w_ref, *rest):
    out_ref, sums_ref = rest[1:] if has_buf else rest
    right = right_ref[...]
    grad = jnp.dot(left_ref[...], right, preferred_element_type=F32)
    out_ref[...] = (w_ref[...].astype(F32) - rate * grad).astype(out_ref.dtype)
    ones = jnp.ones((8, right.shape[0]), right.dtype)
    sums_ref[...] = jnp.dot(ones, right, preferred_element_type=F32)


def update(rate, left, right, weight, first, buf, grant):
    depth, tokens = left.shape
    columns = right.shape[1]
    tile = min(2048, columns)
    base = first // tile
    block = pl.BlockSpec((depth, tile), lambda i: (0, base + i))
    in_specs = [
        pl.BlockSpec((depth, tokens), lambda i: (0, 0)),
        pl.BlockSpec((tokens, tile), lambda i: (0, i)),
        block,
    ]
    args = [left, right, weight]
    if buf is not None:
        in_specs.append(pl.BlockSpec(memory_space=pl.ANY))
        args.append(buf)
    return pl.pallas_call(
        functools.partial(update_kernel, rate, buf is not None),
        grid=(columns // tile,),
        out_shape=(
            jax.ShapeDtypeStruct(weight.shape, weight.dtype),
            jax.ShapeDtypeStruct((8, columns), F32),
        ),
        in_specs=in_specs,
        out_specs=(block, pl.BlockSpec((8, tile), lambda i: (0, i))),
        input_output_aliases={} if buf is None else {3: 0},
        compiler_params=pltpu.CompilerParams(vmem_limit_bytes=grant),
        cost_estimate=pl.CostEstimate(
            flops=2 * depth * tokens * columns, bytes_accessed=4 * depth * columns, transcendentals=0
        ),
    )(*args)


def body(n_latent, n_rows, activations_in, gate_proj, up_proj, down_proj, enc_weight, enc_bias, dec_weight, dec_bias):
    tokens = activations_in.shape[1]
    width, local = enc_weight.shape
    here = activations_in.reshape(tokens, activations_in.shape[2])
    if n_latent == n_rows:
        pairs = [(a * n_rows + b, b * n_rows + a) for a in range(n_latent) for b in range(n_rows)]
        portion = lax.ppermute(here, ("latent", "rows"), pairs)
    else:
        everything = lax.all_gather(here, "latent", axis=1, tiled=True)
        portion = lax.dynamic_slice_in_dim(everything, lax.axis_index("rows") * width, width, 1)
    if n_latent <= 8:
        scatter_l = lambda v, wire: direct_scatter(v, "latent", n_latent, wire)
        gather_l = lambda v: direct_gather(v, "latent", n_latent)
    else:
        scatter_l = lambda v, wire: lax.psum_scatter(v, "latent", scatter_dimension=0, tiled=True)
        gather_l = lambda v: lax.all_gather(v, "latent", axis=0, tiled=True)

    gate_part = jnp.dot(portion, gate_proj, preferred_element_type=F32)
    up_part = jnp.dot(portion, up_proj, preferred_element_type=F32)
    both = jnp.concatenate([gate_part, up_part], axis=1).astype(BF16)
    both = halves_scatter(both, "rows", n_rows, BF16)
    gate_term, up_term = both[:, :gate_proj.shape[1]], both[:, gate_proj.shape[1]:]
    hidden = (jax.nn.gelu(gate_term, approximate=True) * up_term).astype(BF16)
    hidden = halves_gather(hidden, "rows", n_rows)
    partial_value = lax.dot_general(down_proj, hidden, (((0,), (1,)), ((), ())), preferred_element_type=F32)
    inputs_here = scatter_l(partial_value, BF16).astype(BF16)
    inputs = gather_l(inputs_here)
    share = inputs_here.shape[0]
    bias_here = lax.dynamic_slice_in_dim(dec_bias, lax.axis_index("latent") * share, share, 0)

    enc_scale = MODEL_WIDTH ** (-0.5)
    dec_scale = LATENTS ** (-0.5)
    dec_turned = dec_weight.T
    chunks = max(1, min(4, local // 512))
    step = local // chunks
    spans = [slice(c * step, (c + 1) * step) for c in range(chunks)]
    over_width = (((0,), (0,)), ((), ()))
    local_rebuilt = jnp.zeros((width, tokens), F32)
    latents, pres = [], []
    for span in spans:
        part = lax.dot_general(inputs, enc_weight[:, span], over_width, preferred_element_type=F32).astype(BF16)
        encoded = halves_scatter(part, "rows", n_rows, BF16)
        pre = enc_scale * encoded + enc_bias[span]
        pres.append(pre)
        mine = (jax.nn.softplus(sharpness * pre) / sharpness).astype(BF16)
        full = halves_gather(mine, "rows", n_rows)
        latents.append(full)
        local_rebuilt = local_rebuilt + lax.dot_general(
            dec_turned[:, span], full, (((1,), (1,)), ((), ())), preferred_element_type=F32
        )
    rebuilt_share = scatter_l(local_rebuilt, F32)
    grad_share = (
        2.0 * (dec_scale * rebuilt_share + bias_here[:, None] - inputs_here.astype(F32))
    ).astype(BF16)
    residual_grad = gather_l(grad_share)
    grads = []
    for c, span in enumerate(spans):
        part = lax.dot_general(residual_grad, dec_turned[:, span], over_width, preferred_element_type=F32).astype(BF16)
        back = halves_scatter(part, "rows", n_rows, BF16)
        mine = (jax.nn.sigmoid(sharpness * pres[c]) * (dec_scale * back + sparsity_cost)).astype(BF16)
        grads.append(halves_gather(mine, "rows", n_rows))
    dec_new = enc_new = None
    for c, span in enumerate(spans):
        dec_new, _ = update(weight_rate * dec_scale, residual_grad, latents[c], dec_turned, c * step, dec_new, 24 << 20)
    sums = []
    for c, span in enumerate(spans):
        enc_new, total = update(weight_rate * enc_scale, inputs, grads[c], enc_weight, c * step, enc_new, 52 << 20)
        sums.append(total[0])
    enc_bias = enc_bias - enc_bias_rate * jnp.concatenate(sums)
    dec_bias = dec_bias - dec_bias_rate * jnp.sum(residual_grad, axis=1, dtype=F32)
    return (enc_new, enc_bias, dec_new.T, dec_bias)


MESH = pl.DeviceIdType.MESH
HALVES = 2
LEAD = 3
RING = 4


def softplus(v):
    return jnp.maximum(v, 0.0) + jnp.log1p(jnp.exp(-jnp.abs(v)))


def over_last(a, b):
    return lax.dot_general(a, b, (((1,), (1,)), ((), ())), preferred_element_type=F32)


def train_kernel(
    n_latent, n_rows, chunk,
    act_ref, gate_ref, up_ref, down_ref, enc_ref, bias_ref, dec_ref, dec_bias_ref,
    lat_out, grad_out, x_out, resid_out,
    act_turned, act_own, act, gate_up, down, enc, dec,
    ffn_part, ffn_got, ffn_sum, ffn_far, hidden,
    acc, value, value_got, share, features, resid_got, resid_share, resid,
    part, got, pair, far_got, latents, grads,
    load_sem, weight_sem, act_send, act_sem, ffn_send, ffn_sem, z_send, z_sem,
    part_send, part_sem, pair_send, pair_sem, full_send, full_sem, out_sem,
):
    rows = lax.axis_index("rows")
    z = lax.axis_index("latent")
    core = lax.rem(rows, 2)
    mate = {"rows": rows + 1 - 2 * core}
    far = {"rows": lax.rem(rows + 2, n_rows)}
    others = [{"latent": lax.rem(z + s, n_latent)} for s in range(1, n_latent)]
    half = act.shape[1]
    own = half // 2
    small = half // n_latent
    _, local_hidden = gate_ref.shape
    count = enc.shape[0]
    items = HALVES * count
    mine = pl.ds(pl.multiple_of(core * own, own), own)
    theirs = pl.ds(pl.multiple_of((1 - core) * own, own), own)
    small_of = lambda at: pl.ds(pl.multiple_of(at * small, small), small)
    my_small = small_of(z)

    def remote(src, dst, send, recv, to):
        return pltpu.make_async_remote_copy(
            src_ref=src, dst_ref=dst, send_sem=send, recv_sem=recv, device_id=to, device_id_type=MESH
        )

    loads = [
        pltpu.make_async_copy(act_ref, act_turned, load_sem.at[0]),
        pltpu.make_async_copy(gate_ref, gate_up.at[:, :local_hidden], load_sem.at[1]),
        pltpu.make_async_copy(up_ref, gate_up.at[:, local_hidden:], load_sem.at[2]),
        pltpu.make_async_copy(down_ref, down, load_sem.at[3]),
    ]
    for load in loads:
        load.start()
    weights = []
    for c in range(count):
        span = slice(c * chunk, (c + 1) * chunk)
        weights.append(pltpu.make_async_copy(enc_ref.at[:, span], enc.at[c], weight_sem.at[0, c]))
        weights.append(pltpu.make_async_copy(dec_ref.at[:, span], dec.at[c], weight_sem.at[1, c]))
    for load in weights:
        load.start()

    barrier = pltpu.get_barrier_semaphore()
    for to in [mate, far] + others:
        pl.semaphore_signal(barrier, inc=1, device_id=to, device_id_type=MESH)
    loads[0].wait()
    turned = act_turned[...].T
    for h in range(HALVES):
        act_own[h] = turned[h * half:(h + 1) * half]
    pl.semaphore_wait(barrier, n_latent + 1)

    def act_copy(h, s):
        return remote(act_own.at[h], act.at[h], act_send.at[h, s], act_sem.at[h], others[s])

    @pl.when(z == rows)
    def _():
        for h in range(HALVES):
            for s in reversed(range(n_latent - 1)):
                act_copy(h, s).start()
        for h in range(HALVES):
            act[h] = act_own[h]

    @pl.when(z != rows)
    def _():
        act_copy(0, 0).wait_recv()

    loads[1].wait()
    loads[2].wait()

    def ffn_copy(stage, h):
        src, dst, to = (
            (ffn_part.at[h, theirs], ffn_got.at[h], mate),
            (ffn_sum.at[h], ffn_far.at[h], far),
            (hidden.at[h, mine], hidden.at[h, mine], mate),
        )[stage]
        return remote(src, dst, ffn_send.at[stage, h], ffn_sem.at[stage, h], to)

    def z_copies(stage, h):
        copies = []
        for s in range(n_latent - 1):
            to = lax.rem(z + s + 1, n_latent)
            src, dst = (
                (value.at[h, small_of(to)], value_got.at[h, s]),
                (share.at[h], features.at[h, my_small]),
                (acc.at[h, small_of(to)], resid_got.at[h, s]),
                (resid_share.at[h], resid.at[h, my_small]),
            )[stage]
            copies.append(remote(src, dst, z_send.at[stage, h, s], z_sem.at[stage, h, s], others[s]))
        return copies

    for h in range(HALVES):
        if h > 0:
            @pl.when(z != rows)
            def _():
                act_copy(h, 0).wait_recv()
        ffn_part[h] = jnp.dot(act[h], gate_up[...], preferred_element_type=F32).astype(BF16)
        ffn_copy(0, h).start()
    for h in range(HALVES):
        ffn_copy(0, h).wait_recv()
        ffn_sum[h] = (ffn_part[h, mine].astype(F32) + ffn_got[h].astype(F32)).astype(BF16)
        ffn_copy(1, h).start()
    for h in range(HALVES):
        ffn_copy(1, h).wait_recv()
        total = ffn_sum[h].astype(F32) + ffn_far[h].astype(F32)
        gate_term, up_term = total[:, :local_hidden], total[:, local_hidden:]
        hidden[h, mine] = (jax.nn.gelu(gate_term, approximate=True) * up_term).astype(BF16)
        ffn_copy(2, h).start()
    loads[3].wait()
    for h in range(HALVES):
        ffn_copy(2, h).wait_recv()
        part_value = over_last(hidden[h], down[...])
        acc[h] = part_value
        value[h] = part_value.astype(BF16)
        for copy in z_copies(0, h):
            copy.start()
    for h in range(HALVES):
        total = acc[h, my_small]
        for s, copy in enumerate(z_copies(0, h)):
            copy.wait_recv()
            total = total + value_got[h, s].astype(F32)
        share[h] = total.astype(BF16)
        features[h, my_small] = total.astype(BF16)
        for copy in z_copies(1, h):
            copy.start()
        acc[h] = jnp.zeros_like(acc[h])
    for load in weights:
        load.wait()
    for copy in z_copies(1, 0):
        copy.wait_recv()

    enc_scale = MODEL_WIDTH ** (-0.5)
    dec_scale = LATENTS ** (-0.5)

    def near_copy(i):
        slot = lax.rem(i, RING)
        return remote(part.at[slot, theirs], got.at[lax.rem(i, items)], part_send.at[slot], part_sem.at[i], mate)

    def far_copy(i):
        return remote(pair.at[i], far_got.at[i], pair_send.at[i], pair_sem.at[i], far)

    def full_copy(i, full, j):
        return remote(full.at[j, mine], full.at[j, mine], full_send.at[i], full_sem.at[i], mate)

    def out_copy(i, full, j, out):
        h, c = j // count, lax.rem(j, count)
        dst = out.at[
            pl.ds(pl.multiple_of(h * half, half), half), pl.ds(pl.multiple_of(c * chunk, chunk), chunk)
        ]
        return pltpu.make_async_copy(full.at[j], dst, out_sem.at[i])

    def dot_step(i, phase, reuse):
        j = i - phase * items
        h, c = j // count, lax.rem(j, count)
        if reuse:
            near_copy(i - RING).wait_send()
        left, right = ((features, enc), (resid, dec))[phase]
        slot = lax.rem(i, RING)
        part[slot] = jnp.dot(left[h], right[c], preferred_element_type=F32).astype(BF16)
        near_copy(i).start()

    def pair_step(i):
        near_copy(i).wait_recv()
        slot = lax.rem(i, RING)
        pair[i] = (part[slot, mine].astype(F32) + got[lax.rem(i, items)].astype(F32)).astype(BF16)
        far_copy(i).start()

    def pre_of(j):
        return enc_scale * (pair[j].astype(F32) + far_got[j].astype(F32)) + bias_ref[lax.rem(j, count)]

    def full_step(i, phase):
        j = i - phase * items
        far_copy(i).wait_recv()
        if phase == 0:
            latents[j, mine] = (softplus(sharpness * pre_of(j)) / sharpness).astype(BF16)
            full_copy(i, latents, j).start()
        else:
            back = pair[i].astype(F32) + far_got[i].astype(F32)
            slope = jax.nn.sigmoid(sharpness * pre_of(j))
            grads[j, mine] = (slope * (dec_scale * back + sparsity_cost)).astype(BF16)
            full_copy(i, grads, j).start()

    def use_step(i, phase):
        j = i - phase * items
        full, out = ((latents, lat_out), (grads, grad_out))[phase]
        full_copy(i, full, j).wait_recv()
        if phase == 0:
            h, c = j // count, lax.rem(j, count)
            acc[h] += over_last(full[j], dec[c])
        out_copy(i, full, j, out).start()

    def run(first, last):
        if last <= first:
            return

        def body(i, carry):
            if first + LEAD < 2 * items:
                dot_step(i + LEAD, (first + LEAD) // items, True)
            if first + LEAD - 1 < 2 * items:
                pair_step(i + LEAD - 1)
            full_step(i, first // items)
            use_step(i - 1, (first - 1) // items)
            return carry

        lax.fori_loop(first, last, body, 0)

    def resid_step(h):
        total = acc[h, my_small]
        for s, copy in enumerate(z_copies(2, h)):
            copy.wait_recv()
            total = total + resid_got[h, s]
        grad = 2.0 * (dec_scale * total + dec_bias_ref[...] - share[h].astype(F32))
        resid_share[h] = grad.astype(BF16)
        resid[h, my_small] = grad.astype(BF16)
        for copy in z_copies(3, h):
            copy.start()

    for i in range(LEAD):
        dot_step(i, 0, False)
    for i in range(LEAD - 1):
        pair_step(i)
    dot_step(LEAD, 0, LEAD >= RING)
    pair_step(LEAD - 1)
    full_step(0, 0)
    marks = {}
    for h in range(HALVES):
        marks.setdefault((h + 1) * count + 1, []).append(lambda h=h: [copy.start() for copy in z_copies(2, h)])
        marks.setdefault((h + 1) * count + 3, []).append(lambda h=h: resid_step(h))
        marks.setdefault(items + h * count - LEAD, []).append(
            lambda h=h: [copy.wait_recv() for copy in z_copies(3, h)]
        )
        if h > 0:
            marks.setdefault(h * count - LEAD, []).append(lambda h=h: [copy.wait_recv() for copy in z_copies(1, h)])
    cuts = set(marks) | {1, items - LEAD, items - LEAD + 1, items, items + 1}
    cuts |= {2 * items - LEAD, 2 * items - LEAD + 1, 2 * items}
    cuts = sorted(cuts)
    for first, last in zip(cuts[:-1], cuts[1:]):
        for act_on in marks.get(first, []):
            act_on()
        run(first, last)
    use_step(2 * items - 1, 1)

    for h in range(HALVES):
        x_out[h * half:(h + 1) * half] = features[h]
        resid_out[h * half:(h + 1) * half] = resid[h]

    @pl.when(z == rows)
    def _():
        for h in range(HALVES):
            for s in range(n_latent - 1):
                act_copy(h, s).wait_send()

    for h in range(HALVES):
        for stage in range(3):
            ffn_copy(stage, h).wait_send()
        for stage in range(4):
            for copy in z_copies(stage, h):
                copy.wait_send()
    for i in range(2 * items - RING, 2 * items):
        near_copy(i).wait_send()

    def drain(i, carry):
        for phase, full, out in ((0, latents, lat_out), (1, grads, grad_out)):
            at = i + phase * items
            far_copy(at).wait_send()
            full_copy(at, full, i).wait_send()
            out_copy(at, full, i, out).wait()
        return carry

    lax.fori_loop(0, items, drain, 0)


def fast_body(n_latent, n_rows, activations_in, gate_proj, up_proj, down_proj, enc_weight, enc_bias, dec_weight, dec_bias):
    tokens = activations_in.shape[1]
    width, local = enc_weight.shape
    hidden = gate_proj.shape[1]
    chunk = local // CHUNKS
    half = tokens // HALVES
    own, small, items = half // 2, half // n_latent, HALVES * CHUNKS
    dec_turned = dec_weight.T
    any_spec = pl.BlockSpec(memory_space=pl.ANY)
    vmem_spec = pl.BlockSpec(memory_space=pltpu.VMEM)
    vmem, dma = pltpu.VMEM, pltpu.SemaphoreType.DMA
    between = n_latent - 1
    latents, grads, inputs, residual_grad = pl.pallas_call(
        functools.partial(train_kernel, n_latent, n_rows, chunk),
        out_shape=(
            jax.ShapeDtypeStruct((tokens, local), BF16),
            jax.ShapeDtypeStruct((tokens, local), BF16),
            jax.ShapeDtypeStruct((tokens, width), BF16),
            jax.ShapeDtypeStruct((tokens, width), BF16),
        ),
        in_specs=[any_spec] * 5 + [vmem_spec, any_spec, vmem_spec],
        out_specs=(any_spec, any_spec, vmem_spec, vmem_spec),
        scratch_shapes=[
            vmem((width, tokens), BF16),
            vmem((HALVES, half, width), BF16),
            vmem((HALVES, half, width), BF16),
            vmem((width, 2 * hidden), BF16),
            vmem((width, hidden), BF16),
            vmem((CHUNKS, width, chunk), BF16),
            vmem((CHUNKS, width, chunk), BF16),
            vmem((HALVES, half, 2 * hidden), BF16),
            vmem((HALVES, own, 2 * hidden), BF16),
            vmem((HALVES, own, 2 * hidden), BF16),
            vmem((HALVES, own, 2 * hidden), BF16),
            vmem((HALVES, half, hidden), BF16),
            vmem((HALVES, half, width), F32),
            vmem((HALVES, half, width), BF16),
            vmem((HALVES, between, small, width), BF16),
            vmem((HALVES, small, width), BF16),
            vmem((HALVES, half, width), BF16),
            vmem((HALVES, between, small, width), F32),
            vmem((HALVES, small, width), BF16),
            vmem((HALVES, half, width), BF16),
            vmem((RING, half, chunk), BF16),
            vmem((items, own, chunk), BF16),
            vmem((2 * items, own, chunk), BF16),
            vmem((2 * items, own, chunk), BF16),
            vmem((items, half, chunk), BF16),
            vmem((items, half, chunk), BF16),
            dma((4,)),
            dma((2, CHUNKS)),
            dma((HALVES, between)),
            dma((HALVES,)),
            dma((3, HALVES)),
            dma((3, HALVES)),
            dma((4, HALVES, between)),
            dma((4, HALVES, between)),
            dma((RING,)),
            dma((2 * items,)),
            dma((2 * items,)),
            dma((2 * items,)),
            dma((2 * items,)),
            dma((2 * items,)),
            dma((2 * items,)),
        ],
        compiler_params=pltpu.CompilerParams(collective_id=0, has_side_effects=True, vmem_limit_bytes=67043328),
    )(
        activations_in.reshape(tokens, activations_in.shape[2]).T, gate_proj, up_proj, down_proj.T, enc_weight,
        enc_bias.reshape(CHUNKS, 1, chunk), dec_turned, dec_bias.reshape(1, width),
    )
    enc_scale = MODEL_WIDTH ** (-0.5)
    dec_scale = LATENTS ** (-0.5)
    dec_new, _ = update(weight_rate * dec_scale, residual_grad.T, latents, dec_turned, 0, None, 24 << 20)
    enc_new, total = update(weight_rate * enc_scale, inputs.T, grads, enc_weight, 0, None, 24 << 20)
    enc_bias = enc_bias - enc_bias_rate * total[0]
    dec_bias = dec_bias - dec_bias_rate * jnp.sum(residual_grad, axis=0, dtype=F32)
    return (enc_new, enc_bias, dec_new.T, dec_bias)


def solution(mesh):
    def step(*args):
        return run(mesh.shape["latent"], mesh.shape["rows"], *args)

    small = mesh.shape["latent"] == mesh.shape["rows"] == 4
    run = fast_body if small else body


    return jax.shard_map(
        step,
        mesh=mesh,
        in_specs=(
            P("groups", None, "latent"),
            P("rows", "latent"),
            P("rows", "latent"),
            P("latent", "rows"),
            P(("groups", "rows"), "latent"),
            P(("groups", "latent")),
            P(("groups", "latent"), "rows"),
            P(("groups", "rows")),
        ),
        out_specs=(
            P(("groups", "rows"), "latent"),
            P(("groups", "latent")),
            P(("groups", "latent"), "rows"),
            P(("groups", "rows")),
        ),
        check_vma=False,
    )
```

```python
import functools

import jax
import jax.numpy as jnp
from jax import lax
from jax.experimental import pallas as pl
from jax.experimental.pallas import tpu as pltpu
from jax.sharding import PartitionSpec as P

MODEL_WIDTH = 2304
LATENTS = 65536


sparsity_cost = 0.1
sharpness = 8.0
weight_rate = 2.0
enc_bias_rate = 0.01
dec_bias_rate = 0.002

BF16 = jnp.bfloat16
F32 = jnp.float32
CHUNKS = 8
TILE = 256
GRANT = 23 << 20


def swap(x, axis, n, bit):
    return lax.ppermute(x, axis, [(i, i ^ bit) for i in range(n)])


def halves_scatter(x, axis, n, wire):
    me = lax.axis_index(axis)
    bit = 1
    while bit < n:
        size = x.shape[0] // 2
        mine = (me // bit) % 2
        keep = lax.dynamic_slice_in_dim(x, mine * size, size, 0)
        give = lax.dynamic_slice_in_dim(x, (1 - mine) * size, size, 0)
        got = swap(give.astype(wire), axis, n, bit)
        x = keep.astype(F32) + got.astype(F32)
        bit *= 2
    return x


def halves_gather(x, axis, n):
    me = lax.axis_index(axis)
    bit = n // 2
    while bit >= 1:
        got = swap(x, axis, n, bit)
        first = ((me // bit) % 2) == 0
        x = jnp.concatenate([jnp.where(first, x, got), jnp.where(first, got, x)], axis=0)
        bit //= 2
    return x


def direct_scatter(x, axis, n, wire):
    me = lax.axis_index(axis)
    size = x.shape[0] // n
    total = lax.dynamic_slice_in_dim(x, me * size, size, 0)
    gots = []
    for shift in range(1, n):
        to = lax.rem(me + shift, n)
        give = lax.dynamic_slice_in_dim(x, to * size, size, 0).astype(wire)
        gots.append(lax.ppermute(give, axis, [(i, (i + shift) % n) for i in range(n)]))
    for got in gots:
        total = total + got.astype(F32)
    return total


def direct_gather(x, axis, n):
    me = lax.axis_index(axis)
    size = x.shape[0]
    out = jnp.zeros((size * n,) + x.shape[1:], x.dtype)
    parts = [(me, x)]
    for shift in range(1, n):
        got = lax.ppermute(x, axis, [(i, (i + shift) % n) for i in range(n)])
        parts.append((lax.rem(me - shift + n, n), got))
    for at, part in parts:
        out = lax.dynamic_update_slice_in_dim(out, part, at * size, 0)
    return out


def update_kernel(rate, has_buf, left_ref, right_ref, w_ref, *rest):
    out_ref, sums_ref = rest[1:] if has_buf else rest
    right = right_ref[...]
    grad = jnp.dot(left_ref[...], right, preferred_element_type=F32)
    out_ref[...] = (w_ref[...].astype(F32) - rate * grad).astype(out_ref.dtype)
    ones = jnp.ones((8, right.shape[0]), right.dtype)
    sums_ref[...] = jnp.dot(ones, right, preferred_element_type=F32)


def update(rate, left, right, weight, first, buf, grant):
    depth, tokens = left.shape
    columns = right.shape[1]
    tile = min(2048, columns)
    base = first // tile
    block = pl.BlockSpec((depth, tile), lambda i: (0, base + i))
    in_specs = [
        pl.BlockSpec((depth, tokens), lambda i: (0, 0)),
        pl.BlockSpec((tokens, tile), lambda i: (0, i)),
        block,
    ]
    args = [left, right, weight]
    if buf is not None:
        in_specs.append(pl.BlockSpec(memory_space=pl.ANY))
        args.append(buf)
    return pl.pallas_call(
        functools.partial(update_kernel, rate, buf is not None),
        grid=(columns // tile,),
        out_shape=(
            jax.ShapeDtypeStruct(weight.shape, weight.dtype),
            jax.ShapeDtypeStruct((8, columns), F32),
        ),
        in_specs=in_specs,
        out_specs=(block, pl.BlockSpec((8, tile), lambda i: (0, i))),
        input_output_aliases={} if buf is None else {3: 0},
        compiler_params=pltpu.CompilerParams(vmem_limit_bytes=grant),
        cost_estimate=pl.CostEstimate(
            flops=2 * depth * tokens * columns, bytes_accessed=4 * depth * columns, transcendentals=0
        ),
    )(*args)


def body(n_latent, n_rows, activations_in, gate_proj, up_proj, down_proj, enc_weight, enc_bias, dec_weight, dec_bias):
    tokens = activations_in.shape[1]
    width, local = enc_weight.shape
    here = activations_in.reshape(tokens, activations_in.shape[2])
    if n_latent == n_rows:
        pairs = [(a * n_rows + b, b * n_rows + a) for a in range(n_latent) for b in range(n_rows)]
        portion = lax.ppermute(here, ("latent", "rows"), pairs)
    else:
        everything = lax.all_gather(here, "latent", axis=1, tiled=True)
        portion = lax.dynamic_slice_in_dim(everything, lax.axis_index("rows") * width, width, 1)
    if n_latent <= 8:
        scatter_l = lambda v, wire: direct_scatter(v, "latent", n_latent, wire)
        gather_l = lambda v: direct_gather(v, "latent", n_latent)
    else:
        scatter_l = lambda v, wire: lax.psum_scatter(v, "latent", scatter_dimension=0, tiled=True)
        gather_l = lambda v: lax.all_gather(v, "latent", axis=0, tiled=True)

    gate_part = jnp.dot(portion, gate_proj, preferred_element_type=F32)
    up_part = jnp.dot(portion, up_proj, preferred_element_type=F32)
    both = jnp.concatenate([gate_part, up_part], axis=1).astype(BF16)
    both = halves_scatter(both, "rows", n_rows, BF16)
    gate_term, up_term = both[:, :gate_proj.shape[1]], both[:, gate_proj.shape[1]:]
    hidden = (jax.nn.gelu(gate_term, approximate=True) * up_term).astype(BF16)
    hidden = halves_gather(hidden, "rows", n_rows)
    partial_value = lax.dot_general(down_proj, hidden, (((0,), (1,)), ((), ())), preferred_element_type=F32)
    inputs_here = scatter_l(partial_value, BF16).astype(BF16)
    inputs = gather_l(inputs_here)
    share = inputs_here.shape[0]
    bias_here = lax.dynamic_slice_in_dim(dec_bias, lax.axis_index("latent") * share, share, 0)

    enc_scale = MODEL_WIDTH ** (-0.5)
    dec_scale = LATENTS ** (-0.5)
    dec_turned = dec_weight.T
    chunks = max(1, min(4, local // 512))
    step = local // chunks
    spans = [slice(c * step, (c + 1) * step) for c in range(chunks)]
    over_width = (((0,), (0,)), ((), ()))
    local_rebuilt = jnp.zeros((width, tokens), F32)
    latents, pres = [], []
    for span in spans:
        part = lax.dot_general(inputs, enc_weight[:, span], over_width, preferred_element_type=F32).astype(BF16)
        encoded = halves_scatter(part, "rows", n_rows, BF16)
        pre = enc_scale * encoded + enc_bias[span]
        pres.append(pre)
        mine = (jax.nn.softplus(sharpness * pre) / sharpness).astype(BF16)
        full = halves_gather(mine, "rows", n_rows)
        latents.append(full)
        local_rebuilt = local_rebuilt + lax.dot_general(
            dec_turned[:, span], full, (((1,), (1,)), ((), ())), preferred_element_type=F32
        )
    rebuilt_share = scatter_l(local_rebuilt, F32)
    grad_share = (
        2.0 * (dec_scale * rebuilt_share + bias_here[:, None] - inputs_here.astype(F32))
    ).astype(BF16)
    residual_grad = gather_l(grad_share)
    grads = []
    for c, span in enumerate(spans):
        part = lax.dot_general(residual_grad, dec_turned[:, span], over_width, preferred_element_type=F32).astype(BF16)
        back = halves_scatter(part, "rows", n_rows, BF16)
        mine = (jax.nn.sigmoid(sharpness * pres[c]) * (dec_scale * back + sparsity_cost)).astype(BF16)
        grads.append(halves_gather(mine, "rows", n_rows))
    dec_new = enc_new = None
    for c, span in enumerate(spans):
        dec_new, _ = update(weight_rate * dec_scale, residual_grad, latents[c], dec_turned, c * step, dec_new, 24 << 20)
    sums = []
    for c, span in enumerate(spans):
        enc_new, total = update(weight_rate * enc_scale, inputs, grads[c], enc_weight, c * step, enc_new, 52 << 20)
        sums.append(total[0])
    enc_bias = enc_bias - enc_bias_rate * jnp.concatenate(sums)
    dec_bias = dec_bias - dec_bias_rate * jnp.sum(residual_grad, axis=1, dtype=F32)
    return (enc_new, enc_bias, dec_new.T, dec_bias)


MESH = pl.DeviceIdType.MESH
HALVES = 2
LEAD = 3
RING = 4


def softplus(v):
    return jnp.maximum(v, 0.0) + jnp.log1p(jnp.exp(-jnp.abs(v)))


def over_last(a, b):
    return lax.dot_general(a, b, (((1,), (1,)), ((), ())), preferred_element_type=F32)


def train_kernel(
    n_latent, n_rows, chunk,
    act_ref, gate_ref, up_ref, down_ref, enc_ref, bias_ref, dec_ref, dec_bias_ref,
    enc, dec, grads, features, resid,
    act_turned, act_own, act, gate_up, down,
    ffn_part, ffn_got, ffn_sum, ffn_far, hidden,
    acc, value, value_got, share, resid_got, resid_share, resid_turned,
    part, pair, far_got, latents,
    load_sem, weight_sem, act_send, act_sem, ffn_send, ffn_sem, z_send, z_sem,
    part_send, part_sem, pair_send, pair_sem, full_send, full_sem,
):
    rows = lax.axis_index("rows")
    z = lax.axis_index("latent")
    core = lax.rem(rows, 2)
    mate = {"rows": rows + 1 - 2 * core}
    far = {"rows": lax.rem(rows + 2, n_rows)}
    others = [{"latent": lax.rem(z + s, n_latent)} for s in range(1, n_latent)]
    half = act.shape[1]
    own = half // 2
    small = half // n_latent
    _, local_hidden = gate_ref.shape
    count = enc.shape[0]
    items = HALVES * count
    mine = pl.ds(pl.multiple_of(core * own, own), own)
    theirs = pl.ds(pl.multiple_of((1 - core) * own, own), own)
    small_of = lambda at: pl.ds(pl.multiple_of(at * small, small), small)
    my_small = small_of(z)

    def remote(src, dst, send, recv, to):
        return pltpu.make_async_remote_copy(
            src_ref=src, dst_ref=dst, send_sem=send, recv_sem=recv, device_id=to, device_id_type=MESH
        )

    loads = [
        pltpu.make_async_copy(act_ref, act_turned, load_sem.at[0]),
        pltpu.make_async_copy(gate_ref, gate_up.at[:, :local_hidden], load_sem.at[1]),
        pltpu.make_async_copy(up_ref, gate_up.at[:, local_hidden:], load_sem.at[2]),
        pltpu.make_async_copy(down_ref, down, load_sem.at[3]),
    ]
    for load in loads:
        load.start()
    weights = []
    for c in range(count):
        span = slice(c * chunk, (c + 1) * chunk)
        weights.append(pltpu.make_async_copy(enc_ref.at[:, span], enc.at[c], weight_sem.at[0, c]))
        weights.append(pltpu.make_async_copy(dec_ref.at[:, span], dec.at[c], weight_sem.at[1, c]))
    for load in weights:
        load.start()

    barrier = pltpu.get_barrier_semaphore()
    for to in [mate, far] + others:
        pl.semaphore_signal(barrier, inc=1, device_id=to, device_id_type=MESH)
    loads[0].wait()
    turned = act_turned[...].T
    for h in range(HALVES):
        act_own[h] = turned[h * half:(h + 1) * half]
    pl.semaphore_wait(barrier, n_latent + 1)

    def act_copy(h, s):
        return remote(act_own.at[h], act.at[h], act_send.at[h, s], act_sem.at[h], others[s])

    @pl.when(z == rows)
    def _():
        for h in range(HALVES):
            for s in reversed(range(n_latent - 1)):
                act_copy(h, s).start()
        for h in range(HALVES):
            act[h] = act_own[h]

    @pl.when(z != rows)
    def _():
        act_copy(0, 0).wait_recv()

    loads[1].wait()
    loads[2].wait()

    def ffn_copy(stage, h):
        src, dst, to = (
            (ffn_part.at[h, theirs], ffn_got.at[h], mate),
            (ffn_sum.at[h], ffn_far.at[h], far),
            (hidden.at[h, mine], hidden.at[h, mine], mate),
        )[stage]
        return remote(src, dst, ffn_send.at[stage, h], ffn_sem.at[stage, h], to)

    def z_copies(stage, h):
        copies = []
        for s in range(n_latent - 1):
            to = lax.rem(z + s + 1, n_latent)
            src, dst = (
                (value.at[h, small_of(to)], value_got.at[h, s]),
                (share.at[h], features.at[h, my_small]),
                (acc.at[h, small_of(to)], resid_got.at[h, s]),
                (resid_share.at[h], resid.at[h, my_small]),
            )[stage]
            copies.append(remote(src, dst, z_send.at[stage, h, s], z_sem.at[stage, h, s], others[s]))
        return copies

    for h in range(HALVES):
        if h > 0:
            @pl.when(z != rows)
            def _():
                act_copy(h, 0).wait_recv()
        ffn_part[h] = jnp.dot(act[h], gate_up[...], preferred_element_type=F32).astype(BF16)
        ffn_copy(0, h).start()
    for h in range(HALVES):
        ffn_copy(0, h).wait_recv()
        ffn_sum[h] = (ffn_part[h, mine].astype(F32) + ffn_got[h].astype(F32)).astype(BF16)
        ffn_copy(1, h).start()
    for h in range(HALVES):
        ffn_copy(1, h).wait_recv()
        total = ffn_sum[h].astype(F32) + ffn_far[h].astype(F32)
        gate_term, up_term = total[:, :local_hidden], total[:, local_hidden:]
        hidden[h, mine] = (jax.nn.gelu(gate_term, approximate=True) * up_term).astype(BF16)
        ffn_copy(2, h).start()
    loads[3].wait()
    for h in range(HALVES):
        ffn_copy(2, h).wait_recv()
        part_value = over_last(hidden[h], down[...])
        acc[h] = part_value
        value[h] = part_value.astype(BF16)
        for copy in z_copies(0, h):
            copy.start()
    for h in range(HALVES):
        total = acc[h, my_small]
        for s, copy in enumerate(z_copies(0, h)):
            copy.wait_recv()
            total = total + value_got[h, s].astype(F32)
        share[h] = total.astype(BF16)
        features[h, my_small] = total.astype(BF16)
        for copy in z_copies(1, h):
            copy.start()
        acc[h] = jnp.zeros_like(acc[h])
    for load in weights:
        load.wait()
    for copy in z_copies(1, 0):
        copy.wait_recv()

    enc_scale = MODEL_WIDTH ** (-0.5)
    dec_scale = LATENTS ** (-0.5)

    def near_copy(i):
        slot = lax.rem(i, RING)
        return remote(part.at[slot, theirs], grads.at[lax.rem(i, items), theirs], part_send.at[slot], part_sem.at[i], mate)

    def far_copy(i):
        return remote(pair.at[i], far_got.at[i], pair_send.at[i], pair_sem.at[i], far)

    def full_copy(i, full, j):
        return remote(full.at[j, mine], full.at[j, mine], full_send.at[i], full_sem.at[i], mate)

    def dot_step(i, phase, reuse):
        j = i - phase * items
        h, c = j // count, lax.rem(j, count)
        if reuse:
            near_copy(i - RING).wait_send()
        left, right = ((features, enc), (resid, dec))[phase]
        slot = lax.rem(i, RING)
        part[slot] = jnp.dot(left[h], right[c], preferred_element_type=F32).astype(BF16)
        near_copy(i).start()

    def pair_step(i):
        near_copy(i).wait_recv()
        slot = lax.rem(i, RING)
        pair[i] = (part[slot, mine].astype(F32) + grads[lax.rem(i, items), mine].astype(F32)).astype(BF16)
        far_copy(i).start()

    def pre_of(j):
        return enc_scale * (pair[j].astype(F32) + far_got[j].astype(F32)) + bias_ref[lax.rem(j, count)]

    def full_step(i, phase):
        j = i - phase * items
        far_copy(i).wait_recv()
        if phase == 0:
            latents[j, mine] = (softplus(sharpness * pre_of(j)) / sharpness).astype(BF16)
            full_copy(i, latents, j).start()
        else:
            back = pair[i].astype(F32) + far_got[i].astype(F32)
            slope = jax.nn.sigmoid(sharpness * pre_of(j))
            grads[j, mine] = (slope * (dec_scale * back + sparsity_cost)).astype(BF16)
            full_copy(i, grads, j).start()

    def use_step(i, phase):
        j = i - phase * items
        full = (latents, grads)[phase]
        full_copy(i, full, j).wait_recv()
        if phase == 0:
            h, c = j // count, lax.rem(j, count)
            acc[h] += over_last(full[j], dec[c])

    def turn_resid():
        resid_turned[...] = jnp.concatenate([resid[h] for h in range(HALVES)], axis=0).T

    def dec_step(c):
        def tile_step(t, carry):
            span = pl.ds(pl.multiple_of(t * TILE, TILE), TILE)
            right = jnp.concatenate([latents[h * count + c, :, span] for h in range(HALVES)], axis=0)
            grad = jnp.dot(resid_turned[...], right, preferred_element_type=F32)
            dec[c, :, span] = (dec[c, :, span].astype(F32) - weight_rate * dec_scale * grad).astype(BF16)
            return carry

        lax.fori_loop(0, chunk // TILE, tile_step, 0)

    last_dots = 2 * items - count - LEAD + 1

    def run(first, last):
        if last <= first:
            return

        def body(i, carry):
            if first + LEAD < 2 * items:
                dot_step(i + LEAD, (first + LEAD) // items, True)
            if first + LEAD - 1 < 2 * items:
                pair_step(i + LEAD - 1)
            full_step(i, first // items)
            use_step(i - 1, (first - 1) // items)
            if last_dots <= first < last_dots + count:
                dec_step(i - last_dots)
            return carry

        lax.fori_loop(first, last, body, 0)

    def resid_step(h):
        total = acc[h, my_small]
        for s, copy in enumerate(z_copies(2, h)):
            copy.wait_recv()
            total = total + resid_got[h, s]
        grad = 2.0 * (dec_scale * total + dec_bias_ref[...] - share[h].astype(F32))
        resid_share[h] = grad.astype(BF16)
        resid[h, my_small] = grad.astype(BF16)
        for copy in z_copies(3, h):
            copy.start()

    for i in range(LEAD):
        dot_step(i, 0, False)
    for i in range(LEAD - 1):
        pair_step(i)
    dot_step(LEAD, 0, LEAD >= RING)
    pair_step(LEAD - 1)
    full_step(0, 0)
    marks = {}
    for h in range(HALVES):
        marks.setdefault((h + 1) * count + 1, []).append(lambda h=h: [copy.start() for copy in z_copies(2, h)])
        marks.setdefault((h + 1) * count + 3, []).append(lambda h=h: resid_step(h))
        marks.setdefault(items + h * count - LEAD, []).append(
            lambda h=h: [copy.wait_recv() for copy in z_copies(3, h)]
        )
        if h > 0:
            marks.setdefault(h * count - LEAD, []).append(lambda h=h: [copy.wait_recv() for copy in z_copies(1, h)])
    marks.setdefault(last_dots, []).append(turn_resid)
    cuts = set(marks) | {1, items - LEAD, items - LEAD + 1, items, items + 1}
    cuts |= {2 * items - LEAD, 2 * items - LEAD + 1, last_dots + count, 2 * items}
    cuts = sorted(cuts)
    for first, last in zip(cuts[:-1], cuts[1:]):
        for act_on in marks.get(first, []):
            act_on()
        run(first, last)
    use_step(2 * items - 1, 1)

    @pl.when(z == rows)
    def _():
        for h in range(HALVES):
            for s in range(n_latent - 1):
                act_copy(h, s).wait_send()

    for h in range(HALVES):
        for stage in range(3):
            ffn_copy(stage, h).wait_send()
        for stage in range(4):
            for copy in z_copies(stage, h):
                copy.wait_send()
    for i in range(2 * items - RING, 2 * items):
        near_copy(i).wait_send()

    def drain(i, carry):
        for phase, full in ((0, latents), (1, grads)):
            at = i + phase * items
            far_copy(at).wait_send()
            full_copy(at, full, i).wait_send()
        return carry

    lax.fori_loop(0, items, drain, 0)


def write_kernel(
    enc, dec, grads, features, resid, bias_ref, dec_bias_ref, enc_out, dec_out, bias_out, dec_bias_out,
    turned, staged, enc_sem, dec_sem,
):
    count, _, chunk = enc.shape
    enc_rate = weight_rate * MODEL_WIDTH ** (-0.5)

    def out_copies(c):
        span = slice(c * chunk, (c + 1) * chunk)
        return (
            pltpu.make_async_copy(dec.at[c], dec_out.at[:, span], dec_sem.at[c]),
            pltpu.make_async_copy(staged.at[c % RING], enc_out.at[:, span], enc_sem.at[c]),
        )

    copies = [out_copies(c) for c in range(count)]
    turned[...] = jnp.concatenate([features[h] for h in range(HALVES)], axis=0).T
    for c in range(count):
        copies[c][0].start()
        if c >= RING:
            copies[c - RING][1].wait()

        def tile_step(t, carry):
            span = pl.ds(pl.multiple_of(t * TILE, TILE), TILE)
            right = jnp.concatenate([grads[h * count + c, :, span] for h in range(HALVES)], axis=0)
            grad = jnp.dot(turned[...], right, preferred_element_type=F32)
            staged[c % RING, :, span] = (enc[c, :, span].astype(F32) - enc_rate * grad).astype(BF16)
            total = jnp.sum(right.astype(F32), axis=0, keepdims=True)
            bias_out[c, :, span] = bias_ref[c, :, span] - enc_bias_rate * total
            return carry

        lax.fori_loop(0, chunk // TILE, tile_step, 0)
        copies[c][1].start()
    total = sum(jnp.sum(resid[h].astype(F32), axis=0, keepdims=True) for h in range(HALVES))
    dec_bias_out[...] = dec_bias_ref[...] - dec_bias_rate * total
    for c in range(count):
        copies[c][0].wait()
        if c >= count - RING:
            copies[c][1].wait()


def fast_body(n_latent, n_rows, activations_in, gate_proj, up_proj, down_proj, enc_weight, enc_bias, dec_weight, dec_bias):
    tokens = activations_in.shape[1]
    width, local = enc_weight.shape
    hidden = gate_proj.shape[1]
    chunk = local // CHUNKS
    half = tokens // HALVES
    own, small, items = half // 2, half // n_latent, HALVES * CHUNKS
    dec_turned = dec_weight.T
    any_spec = pl.BlockSpec(memory_space=pl.ANY)
    vmem_spec = pl.BlockSpec(memory_space=pltpu.VMEM)
    vmem, dma = pltpu.VMEM, pltpu.SemaphoreType.DMA
    between = n_latent - 1
    enc_held, dec_held, grads, inputs, residual_grad = pl.pallas_call(
        functools.partial(train_kernel, n_latent, n_rows, chunk),
        out_shape=(
            vmem((CHUNKS, width, chunk), BF16),
            vmem((CHUNKS, width, chunk), BF16),
            vmem((items, half, chunk), BF16),
            vmem((HALVES, half, width), BF16),
            vmem((HALVES, half, width), BF16),
        ),
        in_specs=[any_spec] * 5 + [vmem_spec, any_spec, vmem_spec],
        out_specs=(vmem_spec,) * 5,
        scratch_shapes=[
            vmem((width, tokens), BF16),
            vmem((HALVES, half, width), BF16),
            vmem((HALVES, half, width), BF16),
            vmem((width, 2 * hidden), BF16),
            vmem((width, hidden), BF16),
            vmem((HALVES, half, 2 * hidden), BF16),
            vmem((HALVES, own, 2 * hidden), BF16),
            vmem((HALVES, own, 2 * hidden), BF16),
            vmem((HALVES, own, 2 * hidden), BF16),
            vmem((HALVES, half, hidden), BF16),
            vmem((HALVES, half, width), F32),
            vmem((HALVES, half, width), BF16),
            vmem((HALVES, between, small, width), BF16),
            vmem((HALVES, small, width), BF16),
            vmem((HALVES, between, small, width), F32),
            vmem((HALVES, small, width), BF16),
            vmem((width, tokens), BF16),
            vmem((RING, half, chunk), BF16),
            vmem((2 * items, own, chunk), BF16),
            vmem((2 * items, own, chunk), BF16),
            vmem((items, half, chunk), BF16),
            dma((4,)),
            dma((2, CHUNKS)),
            dma((HALVES, between)),
            dma((HALVES,)),
            dma((3, HALVES)),
            dma((3, HALVES)),
            dma((4, HALVES, between)),
            dma((4, HALVES, between)),
            dma((RING,)),
            dma((2 * items,)),
            dma((2 * items,)),
            dma((2 * items,)),
            dma((2 * items,)),
            dma((2 * items,)),
        ],
        compiler_params=pltpu.CompilerParams(collective_id=0, has_side_effects=True, vmem_limit_bytes=GRANT),
    )(
        activations_in.reshape(tokens, activations_in.shape[2]).T, gate_proj, up_proj, down_proj.T, enc_weight,
        enc_bias.reshape(CHUNKS, 1, chunk), dec_turned, dec_bias.reshape(1, width),
    )
    enc_held, dec_held, grads, inputs, residual_grad = (
        pltpu.with_memory_space_constraint(v, vmem) for v in (enc_held, dec_held, grads, inputs, residual_grad)
    )
    enc_new, dec_new, enc_bias, dec_bias = pl.pallas_call(
        write_kernel,
        out_shape=(
            jax.ShapeDtypeStruct((width, local), BF16),
            jax.ShapeDtypeStruct((width, local), BF16),
            jax.ShapeDtypeStruct((CHUNKS, 1, chunk), F32),
            jax.ShapeDtypeStruct((1, width), F32),
        ),
        in_specs=[vmem_spec] * 7,
        out_specs=(any_spec, any_spec, vmem_spec, vmem_spec),
        scratch_shapes=[
            vmem((width, tokens), BF16),
            vmem((RING, width, chunk), BF16),
            dma((CHUNKS,)),
            dma((CHUNKS,)),
        ],
        compiler_params=pltpu.CompilerParams(vmem_limit_bytes=GRANT),
    )(enc_held, dec_held, grads, inputs, residual_grad, enc_bias.reshape(CHUNKS, 1, chunk), dec_bias.reshape(1, width))
    return (enc_new, enc_bias.reshape(local), dec_new.T, dec_bias.reshape(width))


def solution(mesh):
    def step(*args):
        return run(mesh.shape["latent"], mesh.shape["rows"], *args)

    small = mesh.shape["latent"] == mesh.shape["rows"] == 4
    run = fast_body if small else body


    return jax.shard_map(
        step,
        mesh=mesh,
        in_specs=(
            P("groups", None, "latent"),
            P("rows", "latent"),
            P("rows", "latent"),
            P("latent", "rows"),
            P(("groups", "rows"), "latent"),
            P(("groups", "latent")),
            P(("groups", "latent"), "rows"),
            P(("groups", "rows")),
        ),
        out_specs=(
            P(("groups", "rows"), "latent"),
            P(("groups", "latent")),
            P(("groups", "latent"), "rows"),
            P(("groups", "rows")),
        ),
        check_vma=False,
    )
```

```python
import functools

import jax
import jax.numpy as jnp
from jax import lax
from jax.experimental import pallas as pl
from jax.experimental.pallas import tpu as pltpu
from jax.sharding import PartitionSpec as P

MODEL_WIDTH = 2304
LATENTS = 65536


sparsity_cost = 0.1
sharpness = 8.0
weight_rate = 2.0
enc_bias_rate = 0.01
dec_bias_rate = 0.002

BF16 = jnp.bfloat16
F32 = jnp.float32
CHUNKS = 8
TILE = 256
WIDE = 1024
GRANT = 23 << 20


def swap(x, axis, n, bit):
    return lax.ppermute(x, axis, [(i, i ^ bit) for i in range(n)])


def halves_scatter(x, axis, n, wire):
    me = lax.axis_index(axis)
    bit = 1
    while bit < n:
        size = x.shape[0] // 2
        mine = (me // bit) % 2
        keep = lax.dynamic_slice_in_dim(x, mine * size, size, 0)
        give = lax.dynamic_slice_in_dim(x, (1 - mine) * size, size, 0)
        got = swap(give.astype(wire), axis, n, bit)
        x = keep.astype(F32) + got.astype(F32)
        bit *= 2
    return x


def halves_gather(x, axis, n):
    me = lax.axis_index(axis)
    bit = n // 2
    while bit >= 1:
        got = swap(x, axis, n, bit)
        first = ((me // bit) % 2) == 0
        x = jnp.concatenate([jnp.where(first, x, got), jnp.where(first, got, x)], axis=0)
        bit //= 2
    return x


def direct_scatter(x, axis, n, wire):
    me = lax.axis_index(axis)
    size = x.shape[0] // n
    total = lax.dynamic_slice_in_dim(x, me * size, size, 0)
    gots = []
    for shift in range(1, n):
        to = lax.rem(me + shift, n)
        give = lax.dynamic_slice_in_dim(x, to * size, size, 0).astype(wire)
        gots.append(lax.ppermute(give, axis, [(i, (i + shift) % n) for i in range(n)]))
    for got in gots:
        total = total + got.astype(F32)
    return total


def direct_gather(x, axis, n):
    me = lax.axis_index(axis)
    size = x.shape[0]
    out = jnp.zeros((size * n,) + x.shape[1:], x.dtype)
    parts = [(me, x)]
    for shift in range(1, n):
        got = lax.ppermute(x, axis, [(i, (i + shift) % n) for i in range(n)])
        parts.append((lax.rem(me - shift + n, n), got))
    for at, part in parts:
        out = lax.dynamic_update_slice_in_dim(out, part, at * size, 0)
    return out


def update_kernel(rate, has_buf, left_ref, right_ref, w_ref, *rest):
    out_ref, sums_ref = rest[1:] if has_buf else rest
    right = right_ref[...]
    grad = jnp.dot(left_ref[...], right, preferred_element_type=F32)
    out_ref[...] = (w_ref[...].astype(F32) - rate * grad).astype(out_ref.dtype)
    ones = jnp.ones((8, right.shape[0]), right.dtype)
    sums_ref[...] = jnp.dot(ones, right, preferred_element_type=F32)


def update(rate, left, right, weight, first, buf, grant):
    depth, tokens = left.shape
    columns = right.shape[1]
    tile = min(2048, columns)
    base = first // tile
    block = pl.BlockSpec((depth, tile), lambda i: (0, base + i))
    in_specs = [
        pl.BlockSpec((depth, tokens), lambda i: (0, 0)),
        pl.BlockSpec((tokens, tile), lambda i: (0, i)),
        block,
    ]
    args = [left, right, weight]
    if buf is not None:
        in_specs.append(pl.BlockSpec(memory_space=pl.ANY))
        args.append(buf)
    return pl.pallas_call(
        functools.partial(update_kernel, rate, buf is not None),
        grid=(columns // tile,),
        out_shape=(
            jax.ShapeDtypeStruct(weight.shape, weight.dtype),
            jax.ShapeDtypeStruct((8, columns), F32),
        ),
        in_specs=in_specs,
        out_specs=(block, pl.BlockSpec((8, tile), lambda i: (0, i))),
        input_output_aliases={} if buf is None else {3: 0},
        compiler_params=pltpu.CompilerParams(vmem_limit_bytes=grant),
        cost_estimate=pl.CostEstimate(
            flops=2 * depth * tokens * columns, bytes_accessed=4 * depth * columns, transcendentals=0
        ),
    )(*args)


def body(n_latent, n_rows, activations_in, gate_proj, up_proj, down_proj, enc_weight, enc_bias, dec_weight, dec_bias):
    tokens = activations_in.shape[1]
    width, local = enc_weight.shape
    here = activations_in.reshape(tokens, activations_in.shape[2])
    if n_latent == n_rows:
        pairs = [(a * n_rows + b, b * n_rows + a) for a in range(n_latent) for b in range(n_rows)]
        portion = lax.ppermute(here, ("latent", "rows"), pairs)
    else:
        everything = lax.all_gather(here, "latent", axis=1, tiled=True)
        portion = lax.dynamic_slice_in_dim(everything, lax.axis_index("rows") * width, width, 1)
    if n_latent <= 8:
        scatter_l = lambda v, wire: direct_scatter(v, "latent", n_latent, wire)
        gather_l = lambda v: direct_gather(v, "latent", n_latent)
    else:
        scatter_l = lambda v, wire: lax.psum_scatter(v, "latent", scatter_dimension=0, tiled=True)
        gather_l = lambda v: lax.all_gather(v, "latent", axis=0, tiled=True)

    gate_part = jnp.dot(portion, gate_proj, preferred_element_type=F32)
    up_part = jnp.dot(portion, up_proj, preferred_element_type=F32)
    both = jnp.concatenate([gate_part, up_part], axis=1).astype(BF16)
    both = halves_scatter(both, "rows", n_rows, BF16)
    gate_term, up_term = both[:, :gate_proj.shape[1]], both[:, gate_proj.shape[1]:]
    hidden = (jax.nn.gelu(gate_term, approximate=True) * up_term).astype(BF16)
    hidden = halves_gather(hidden, "rows", n_rows)
    partial_value = lax.dot_general(down_proj, hidden, (((0,), (1,)), ((), ())), preferred_element_type=F32)
    inputs_here = scatter_l(partial_value, BF16).astype(BF16)
    inputs = gather_l(inputs_here)
    share = inputs_here.shape[0]
    bias_here = lax.dynamic_slice_in_dim(dec_bias, lax.axis_index("latent") * share, share, 0)

    enc_scale = MODEL_WIDTH ** (-0.5)
    dec_scale = LATENTS ** (-0.5)
    dec_turned = dec_weight.T
    chunks = max(1, min(4, local // 512))
    step = local // chunks
    spans = [slice(c * step, (c + 1) * step) for c in range(chunks)]
    over_width = (((0,), (0,)), ((), ()))
    local_rebuilt = jnp.zeros((width, tokens), F32)
    latents, pres = [], []
    for span in spans:
        part = lax.dot_general(inputs, enc_weight[:, span], over_width, preferred_element_type=F32).astype(BF16)
        encoded = halves_scatter(part, "rows", n_rows, BF16)
        pre = enc_scale * encoded + enc_bias[span]
        pres.append(pre)
        mine = (jax.nn.softplus(sharpness * pre) / sharpness).astype(BF16)
        full = halves_gather(mine, "rows", n_rows)
        latents.append(full)
        local_rebuilt = local_rebuilt + lax.dot_general(
            dec_turned[:, span], full, (((1,), (1,)), ((), ())), preferred_element_type=F32
        )
    rebuilt_share = scatter_l(local_rebuilt, F32)
    grad_share = (
        2.0 * (dec_scale * rebuilt_share + bias_here[:, None] - inputs_here.astype(F32))
    ).astype(BF16)
    residual_grad = gather_l(grad_share)
    grads = []
    for c, span in enumerate(spans):
        part = lax.dot_general(residual_grad, dec_turned[:, span], over_width, preferred_element_type=F32).astype(BF16)
        back = halves_scatter(part, "rows", n_rows, BF16)
        mine = (jax.nn.sigmoid(sharpness * pres[c]) * (dec_scale * back + sparsity_cost)).astype(BF16)
        grads.append(halves_gather(mine, "rows", n_rows))
    dec_new = enc_new = None
    for c, span in enumerate(spans):
        dec_new, _ = update(weight_rate * dec_scale, residual_grad, latents[c], dec_turned, c * step, dec_new, 24 << 20)
    sums = []
    for c, span in enumerate(spans):
        enc_new, total = update(weight_rate * enc_scale, inputs, grads[c], enc_weight, c * step, enc_new, 52 << 20)
        sums.append(total[0])
    enc_bias = enc_bias - enc_bias_rate * jnp.concatenate(sums)
    dec_bias = dec_bias - dec_bias_rate * jnp.sum(residual_grad, axis=1, dtype=F32)
    return (enc_new, enc_bias, dec_new.T, dec_bias)


MESH = pl.DeviceIdType.MESH
HALVES = 2
LEAD = 3
RING = 4
STAGED = 4


def softplus(v):
    return jnp.maximum(v, 0.0) + jnp.log1p(jnp.exp(-jnp.abs(v)))


def over_last(a, b):
    return lax.dot_general(a, b, (((1,), (1,)), ((), ())), preferred_element_type=F32)


def train_kernel(
    n_latent, n_rows, chunk,
    act_ref, gate_ref, up_ref, down_ref, enc_ref, bias_ref, dec_ref, dec_bias_ref,
    enc, dec, grads, features, resid,
    act_turned, act_own, act, gate_up, down,
    ffn_part, ffn_got, ffn_sum, ffn_far, hidden,
    acc, value, value_got, share, resid_got, resid_share, resid_turned,
    part, pair, far_got, latents,
    load_sem, weight_sem, act_send, act_sem, ffn_send, ffn_sem, z_send, z_sem,
    part_send, part_sem, pair_send, pair_sem, full_send, full_sem,
):
    rows = lax.axis_index("rows")
    z = lax.axis_index("latent")
    core = lax.rem(rows, 2)
    mate = {"rows": rows + 1 - 2 * core}
    far = {"rows": lax.rem(rows + 2, n_rows)}
    others = [{"latent": lax.rem(z + s, n_latent)} for s in range(1, n_latent)]
    half = act.shape[1]
    own = half // 2
    small = half // n_latent
    width, local_hidden = gate_ref.shape
    count = enc.shape[0]
    items = HALVES * count
    mine = pl.ds(pl.multiple_of(core * own, own), own)
    theirs = pl.ds(pl.multiple_of((1 - core) * own, own), own)
    small_of = lambda at: pl.ds(pl.multiple_of(at * small, small), small)
    my_small = small_of(z)

    def remote(src, dst, send, recv, to):
        return pltpu.make_async_remote_copy(
            src_ref=src, dst_ref=dst, send_sem=send, recv_sem=recv, device_id=to, device_id_type=MESH
        )

    loads = [
        pltpu.make_async_copy(act_ref, act_turned, load_sem.at[0]),
        pltpu.make_async_copy(gate_ref, gate_up.at[:, :local_hidden], load_sem.at[1]),
        pltpu.make_async_copy(up_ref, gate_up.at[:, local_hidden:], load_sem.at[2]),
        pltpu.make_async_copy(down_ref, down, load_sem.at[3]),
    ]
    for load in loads:
        load.start()
    weights = []
    for c in range(count):
        span = slice(c * chunk, (c + 1) * chunk)
        weights.append(pltpu.make_async_copy(enc_ref.at[:, span], enc.at[c], weight_sem.at[0, c]))
        weights.append(pltpu.make_async_copy(dec_ref.at[:, span], dec.at[c], weight_sem.at[1, c]))
    for load in weights:
        load.start()

    barrier = pltpu.get_barrier_semaphore()
    for to in [mate, far] + others:
        pl.semaphore_signal(barrier, inc=1, device_id=to, device_id_type=MESH)
    loads[0].wait()
    turned = act_turned[...].T
    for h in range(HALVES):
        act_own[h] = turned[h * half:(h + 1) * half]
    pl.semaphore_wait(barrier, n_latent + 1)

    def act_copy(h, s):
        return remote(act_own.at[h], act.at[h], act_send.at[h, s], act_sem.at[h], others[s])

    @pl.when(z == rows)
    def _():
        for h in range(HALVES):
            for s in reversed(range(n_latent - 1)):
                act_copy(h, s).start()
        for h in range(HALVES):
            act[h] = act_own[h]

    @pl.when(z != rows)
    def _():
        act_copy(0, 0).wait_recv()

    loads[1].wait()
    loads[2].wait()

    def ffn_copy(stage, h):
        src, dst, to = (
            (ffn_part.at[h, theirs], ffn_got.at[h], mate),
            (ffn_sum.at[h], ffn_far.at[h], far),
            (hidden.at[h, mine], hidden.at[h, mine], mate),
        )[stage]
        return remote(src, dst, ffn_send.at[stage, h], ffn_sem.at[stage, h], to)

    def z_copies(stage, h):
        copies = []
        for s in range(n_latent - 1):
            to = lax.rem(z + s + 1, n_latent)
            src, dst = (
                (value.at[h, small_of(to)], value_got.at[h, s]),
                (share.at[h], features.at[h, my_small]),
                (acc.at[h, small_of(to)], resid_got.at[h, s]),
                (resid_share.at[h], resid.at[h, my_small]),
            )[stage]
            copies.append(remote(src, dst, z_send.at[stage, h, s], z_sem.at[stage, h, s], others[s]))
        return copies

    for h in range(HALVES):
        if h > 0:
            @pl.when(z != rows)
            def _():
                act_copy(h, 0).wait_recv()
        ffn_part[h] = jnp.dot(act[h], gate_up[...], preferred_element_type=F32).astype(BF16)
        ffn_copy(0, h).start()
    for h in range(HALVES):
        ffn_copy(0, h).wait_recv()
        ffn_sum[h] = (ffn_part[h, mine].astype(F32) + ffn_got[h].astype(F32)).astype(BF16)
        ffn_copy(1, h).start()
    for h in range(HALVES):
        ffn_copy(1, h).wait_recv()
        total = ffn_sum[h].astype(F32) + ffn_far[h].astype(F32)
        gate_term, up_term = total[:, :local_hidden], total[:, local_hidden:]
        hidden[h, mine] = (jax.nn.gelu(gate_term, approximate=True) * up_term).astype(BF16)
        ffn_copy(2, h).start()
    loads[3].wait()
    for h in range(HALVES):
        ffn_copy(2, h).wait_recv()
        part_value = over_last(hidden[h], down[...])
        acc[h] = part_value
        value[h] = part_value.astype(BF16)
        for copy in z_copies(0, h):
            copy.start()
    for h in range(HALVES):
        total = acc[h, my_small]
        for s, copy in enumerate(z_copies(0, h)):
            copy.wait_recv()
            total = total + value_got[h, s].astype(F32)
        share[h] = total.astype(BF16)
        features[h, my_small] = total.astype(BF16)
        for copy in z_copies(1, h):
            copy.start()
        acc[h] = jnp.zeros_like(acc[h])
    for load in weights:
        load.wait()
    for copy in z_copies(1, 0):
        copy.wait_recv()

    enc_scale = MODEL_WIDTH ** (-0.5)
    dec_scale = LATENTS ** (-0.5)

    def near_copy(i):
        slot = lax.rem(i, RING)
        return remote(part.at[slot, theirs], grads.at[lax.rem(i, items), theirs], part_send.at[slot], part_sem.at[i], mate)

    def far_copy(i):
        return remote(pair.at[i], far_got.at[i], pair_send.at[i], pair_sem.at[i], far)

    def full_copy(i, full, j):
        return remote(full.at[j, mine], full.at[j, mine], full_send.at[i], full_sem.at[i], mate)

    def dot_step(i, phase, reuse):
        j = i - phase * items
        h, c = j // count, lax.rem(j, count)
        if reuse:
            near_copy(i - RING).wait_send()
        left, right = ((features, enc), (resid, dec))[phase]
        slot = lax.rem(i, RING)
        part[slot] = jnp.dot(left[h], right[c], preferred_element_type=F32).astype(BF16)
        near_copy(i).start()

    def pair_step(i):
        near_copy(i).wait_recv()
        slot = lax.rem(i, RING)
        pair[i] = (part[slot, mine].astype(F32) + grads[lax.rem(i, items), mine].astype(F32)).astype(BF16)
        far_copy(i).start()

    def pre_of(j):
        return enc_scale * (pair[j].astype(F32) + far_got[j].astype(F32)) + bias_ref[lax.rem(j, count)]

    def full_step(i, phase):
        j = i - phase * items
        far_copy(i).wait_recv()
        if phase == 0:
            latents[j, mine] = (softplus(sharpness * pre_of(j)) / sharpness).astype(BF16)
            full_copy(i, latents, j).start()
        else:
            back = pair[i].astype(F32) + far_got[i].astype(F32)
            slope = jax.nn.sigmoid(sharpness * pre_of(j))
            grads[j, mine] = (slope * (dec_scale * back + sparsity_cost)).astype(BF16)
            full_copy(i, grads, j).start()

    def use_step(i, phase):
        j = i - phase * items
        full = (latents, grads)[phase]
        full_copy(i, full, j).wait_recv()
        if phase == 0:
            h, c = j // count, lax.rem(j, count)
            acc[h] += over_last(full[j], dec[c])

    def turn_resid():
        resid_turned[...] = jnp.concatenate([resid[h] for h in range(HALVES)], axis=0).T

    def dec_step(c):
        def tile_step(t, carry):
            span = pl.ds(pl.multiple_of(t * TILE, TILE), TILE)
            right = jnp.concatenate([latents[h * count + c, :, span] for h in range(HALVES)], axis=0)
            grad = jnp.dot(resid_turned[...], right, preferred_element_type=F32)
            dec[c, :, span] = (dec[c, :, span].astype(F32) - weight_rate * dec_scale * grad).astype(BF16)
            return carry

        lax.fori_loop(0, chunk // TILE, tile_step, 0)

    last_dots = 2 * items - count - LEAD + 1

    def run(first, last):
        if last <= first:
            return

        def body(i, carry):
            if first + LEAD < 2 * items:
                dot_step(i + LEAD, (first + LEAD) // items, True)
            if first + LEAD - 1 < 2 * items:
                pair_step(i + LEAD - 1)
            full_step(i, first // items)
            use_step(i - 1, (first - 1) // items)
            if last_dots <= first < last_dots + count:
                dec_step(i - last_dots)
            return carry

        lax.fori_loop(first, last, body, 0)

    def resid_step(h):
        total = acc[h, my_small]
        for s, copy in enumerate(z_copies(2, h)):
            copy.wait_recv()
            total = total + resid_got[h, s]
        grad = 2.0 * (dec_scale * total + dec_bias_ref[...].reshape(1, width) - share[h].astype(F32))
        resid_share[h] = grad.astype(BF16)
        resid[h, my_small] = grad.astype(BF16)
        for copy in z_copies(3, h):
            copy.start()

    for i in range(LEAD):
        dot_step(i, 0, False)
    for i in range(LEAD - 1):
        pair_step(i)
    dot_step(LEAD, 0, LEAD >= RING)
    pair_step(LEAD - 1)
    full_step(0, 0)
    marks = {}
    for h in range(HALVES):
        marks.setdefault((h + 1) * count + 1, []).append(lambda h=h: [copy.start() for copy in z_copies(2, h)])
        marks.setdefault((h + 1) * count + 3, []).append(lambda h=h: resid_step(h))
        marks.setdefault(items + h * count - LEAD, []).append(
            lambda h=h: [copy.wait_recv() for copy in z_copies(3, h)]
        )
        if h > 0:
            marks.setdefault(h * count - LEAD, []).append(lambda h=h: [copy.wait_recv() for copy in z_copies(1, h)])
    marks.setdefault(last_dots, []).append(turn_resid)
    cuts = set(marks) | {1, items - LEAD, items - LEAD + 1, items, items + 1}
    cuts |= {2 * items - LEAD, 2 * items - LEAD + 1, last_dots + count, 2 * items}
    cuts = sorted(cuts)
    for first, last in zip(cuts[:-1], cuts[1:]):
        for act_on in marks.get(first, []):
            act_on()
        run(first, last)
    use_step(2 * items - 1, 1)

    @pl.when(z == rows)
    def _():
        for h in range(HALVES):
            for s in range(n_latent - 1):
                act_copy(h, s).wait_send()

    for h in range(HALVES):
        for stage in range(3):
            ffn_copy(stage, h).wait_send()
        for stage in range(4):
            for copy in z_copies(stage, h):
                copy.wait_send()
    for i in range(2 * items - RING, 2 * items):
        near_copy(i).wait_send()

    def drain(i, carry):
        for phase, full in ((0, latents), (1, grads)):
            at = i + phase * items
            far_copy(at).wait_send()
            full_copy(at, full, i).wait_send()
        return carry

    lax.fori_loop(0, items, drain, 0)


def write_kernel(
    enc, dec, grads, features, resid, bias_ref, dec_bias_ref, enc_out, dec_out, bias_out, dec_bias_out,
    turned, staged, enc_sem, dec_sem,
):
    count, _, chunk = enc.shape
    enc_rate = weight_rate * MODEL_WIDTH ** (-0.5)

    def out_copies(c):
        span = slice(c * chunk, (c + 1) * chunk)
        return (
            pltpu.make_async_copy(dec.at[c], dec_out.at[:, span], dec_sem.at[c]),
            pltpu.make_async_copy(staged.at[c % STAGED], enc_out.at[:, span], enc_sem.at[c]),
        )

    copies = [out_copies(c) for c in range(count)]
    turned[...] = jnp.concatenate([features[h] for h in range(HALVES)], axis=0).T
    for c in range(count):
        copies[c][0].start()
        if c >= STAGED:
            copies[c - STAGED][1].wait()

        def tile_step(t, carry):
            span = pl.ds(pl.multiple_of(t * WIDE, WIDE), WIDE)
            right = jnp.concatenate([grads[h * count + c, :, span] for h in range(HALVES)], axis=0)
            grad = jnp.dot(turned[...], right, preferred_element_type=F32)
            staged[c % STAGED, :, span] = (enc[c, :, span].astype(F32) - enc_rate * grad).astype(BF16)
            total = jnp.sum(right.astype(F32), axis=0, keepdims=True)
            bias_out[c, :, span] = bias_ref[c, :, span] - enc_bias_rate * total
            return carry

        lax.fori_loop(0, chunk // WIDE, tile_step, 0)
        copies[c][1].start()
    total = sum(jnp.sum(resid[h].astype(F32), axis=0) for h in range(HALVES))
    dec_bias_out[...] = dec_bias_ref[...] - dec_bias_rate * total
    for c in range(count):
        copies[c][0].wait()
        if c >= count - STAGED:
            copies[c][1].wait()


def fast_body(n_latent, n_rows, activations_in, gate_proj, up_proj, down_proj, enc_weight, enc_bias, dec_weight, dec_bias):
    tokens = activations_in.shape[1]
    width, local = enc_weight.shape
    hidden = gate_proj.shape[1]
    chunk = local // CHUNKS
    half = tokens // HALVES
    own, small, items = half // 2, half // n_latent, HALVES * CHUNKS
    dec_turned = dec_weight.T
    any_spec = pl.BlockSpec(memory_space=pl.ANY)
    vmem_spec = pl.BlockSpec(memory_space=pltpu.VMEM)
    vmem, dma = pltpu.VMEM, pltpu.SemaphoreType.DMA
    between = n_latent - 1
    enc_held, dec_held, grads, inputs, residual_grad = pl.pallas_call(
        functools.partial(train_kernel, n_latent, n_rows, chunk),
        out_shape=(
            vmem((CHUNKS, width, chunk), BF16),
            vmem((CHUNKS, width, chunk), BF16),
            vmem((items, half, chunk), BF16),
            vmem((HALVES, half, width), BF16),
            vmem((HALVES, half, width), BF16),
        ),
        in_specs=[any_spec] * 5 + [vmem_spec, any_spec, vmem_spec],
        out_specs=(vmem_spec,) * 5,
        scratch_shapes=[
            vmem((width, tokens), BF16),
            vmem((HALVES, half, width), BF16),
            vmem((HALVES, half, width), BF16),
            vmem((width, 2 * hidden), BF16),
            vmem((width, hidden), BF16),
            vmem((HALVES, half, 2 * hidden), BF16),
            vmem((HALVES, own, 2 * hidden), BF16),
            vmem((HALVES, own, 2 * hidden), BF16),
            vmem((HALVES, own, 2 * hidden), BF16),
            vmem((HALVES, half, hidden), BF16),
            vmem((HALVES, half, width), F32),
            vmem((HALVES, half, width), BF16),
            vmem((HALVES, between, small, width), BF16),
            vmem((HALVES, small, width), BF16),
            vmem((HALVES, between, small, width), F32),
            vmem((HALVES, small, width), BF16),
            vmem((width, tokens), BF16),
            vmem((RING, half, chunk), BF16),
            vmem((2 * items, own, chunk), BF16),
            vmem((2 * items, own, chunk), BF16),
            vmem((items, half, chunk), BF16),
            dma((4,)),
            dma((2, CHUNKS)),
            dma((HALVES, between)),
            dma((HALVES,)),
            dma((3, HALVES)),
            dma((3, HALVES)),
            dma((4, HALVES, between)),
            dma((4, HALVES, between)),
            dma((RING,)),
            dma((2 * items,)),
            dma((2 * items,)),
            dma((2 * items,)),
            dma((2 * items,)),
            dma((2 * items,)),
        ],
        compiler_params=pltpu.CompilerParams(collective_id=0, has_side_effects=True, vmem_limit_bytes=GRANT),
    )(
        activations_in.reshape(tokens, activations_in.shape[2]).T, gate_proj, up_proj, down_proj.T, enc_weight,
        enc_bias.reshape(CHUNKS, 1, chunk), dec_turned, dec_bias,
    )
    enc_held, dec_held, grads, inputs, residual_grad = (
        pltpu.with_memory_space_constraint(v, vmem) for v in (enc_held, dec_held, grads, inputs, residual_grad)
    )
    enc_new, dec_new, enc_bias, dec_bias = pl.pallas_call(
        write_kernel,
        out_shape=(
            jax.ShapeDtypeStruct((width, local), BF16),
            jax.ShapeDtypeStruct((width, local), BF16),
            jax.ShapeDtypeStruct((CHUNKS, 1, chunk), F32),
            jax.ShapeDtypeStruct((width,), F32),
        ),
        in_specs=[vmem_spec] * 7,
        out_specs=(any_spec, any_spec, vmem_spec, vmem_spec),
        scratch_shapes=[
            vmem((width, tokens), BF16),
            vmem((STAGED, width, chunk), BF16),
            dma((CHUNKS,)),
            dma((CHUNKS,)),
        ],
        compiler_params=pltpu.CompilerParams(vmem_limit_bytes=GRANT),
    )(enc_held, dec_held, grads, inputs, residual_grad, enc_bias.reshape(CHUNKS, 1, chunk), dec_bias)
    return (enc_new, enc_bias.reshape(local), dec_new.T, dec_bias)


def solution(mesh):
    def step(*args):
        return run(mesh.shape["latent"], mesh.shape["rows"], *args)

    small = mesh.shape["latent"] == mesh.shape["rows"] == 4
    run = fast_body if small else body


    return jax.shard_map(
        step,
        mesh=mesh,
        in_specs=(
            P("groups", None, "latent"),
            P("rows", "latent"),
            P("rows", "latent"),
            P("latent", "rows"),
            P(("groups", "rows"), "latent"),
            P(("groups", "latent")),
            P(("groups", "latent"), "rows"),
            P(("groups", "rows")),
        ),
        out_specs=(
            P(("groups", "rows"), "latent"),
            P(("groups", "latent")),
            P(("groups", "latent"), "rows"),
            P(("groups", "rows")),
        ),
        check_vma=False,
    )
```

```python
import functools

import jax
import jax.numpy as jnp
from jax import lax
from jax.experimental import pallas as pl
from jax.experimental.pallas import tpu as pltpu
from jax.sharding import PartitionSpec as P

MODEL_WIDTH = 2304
LATENTS = 65536


sparsity_cost = 0.1
sharpness = 8.0
weight_rate = 2.0
enc_bias_rate = 0.01
dec_bias_rate = 0.002

BF16 = jnp.bfloat16
F32 = jnp.float32
CHUNKS = 8
TILE = 256
WIDE = 1024
GRANT = 23 << 20


def swap(x, axis, n, bit):
    return lax.ppermute(x, axis, [(i, i ^ bit) for i in range(n)])


def halves_scatter(x, axis, n, wire):
    me = lax.axis_index(axis)
    bit = 1
    while bit < n:
        size = x.shape[0] // 2
        mine = (me // bit) % 2
        keep = lax.dynamic_slice_in_dim(x, mine * size, size, 0)
        give = lax.dynamic_slice_in_dim(x, (1 - mine) * size, size, 0)
        got = swap(give.astype(wire), axis, n, bit)
        x = keep.astype(F32) + got.astype(F32)
        bit *= 2
    return x


def halves_gather(x, axis, n):
    me = lax.axis_index(axis)
    bit = n // 2
    while bit >= 1:
        got = swap(x, axis, n, bit)
        first = ((me // bit) % 2) == 0
        x = jnp.concatenate([jnp.where(first, x, got), jnp.where(first, got, x)], axis=0)
        bit //= 2
    return x


def direct_scatter(x, axis, n, wire):
    me = lax.axis_index(axis)
    size = x.shape[0] // n
    total = lax.dynamic_slice_in_dim(x, me * size, size, 0)
    gots = []
    for shift in range(1, n):
        to = lax.rem(me + shift, n)
        give = lax.dynamic_slice_in_dim(x, to * size, size, 0).astype(wire)
        gots.append(lax.ppermute(give, axis, [(i, (i + shift) % n) for i in range(n)]))
    for got in gots:
        total = total + got.astype(F32)
    return total


def direct_gather(x, axis, n):
    me = lax.axis_index(axis)
    size = x.shape[0]
    out = jnp.zeros((size * n,) + x.shape[1:], x.dtype)
    parts = [(me, x)]
    for shift in range(1, n):
        got = lax.ppermute(x, axis, [(i, (i + shift) % n) for i in range(n)])
        parts.append((lax.rem(me - shift + n, n), got))
    for at, part in parts:
        out = lax.dynamic_update_slice_in_dim(out, part, at * size, 0)
    return out


def update_kernel(rate, has_buf, left_ref, right_ref, w_ref, *rest):
    out_ref, sums_ref = rest[1:] if has_buf else rest
    right = right_ref[...]
    grad = jnp.dot(left_ref[...], right, preferred_element_type=F32)
    out_ref[...] = (w_ref[...].astype(F32) - rate * grad).astype(out_ref.dtype)
    ones = jnp.ones((8, right.shape[0]), right.dtype)
    sums_ref[...] = jnp.dot(ones, right, preferred_element_type=F32)


def update(rate, left, right, weight, first, buf, grant):
    depth, tokens = left.shape
    columns = right.shape[1]
    tile = min(2048, columns)
    base = first // tile
    block = pl.BlockSpec((depth, tile), lambda i: (0, base + i))
    in_specs = [
        pl.BlockSpec((depth, tokens), lambda i: (0, 0)),
        pl.BlockSpec((tokens, tile), lambda i: (0, i)),
        block,
    ]
    args = [left, right, weight]
    if buf is not None:
        in_specs.append(pl.BlockSpec(memory_space=pl.ANY))
        args.append(buf)
    return pl.pallas_call(
        functools.partial(update_kernel, rate, buf is not None),
        grid=(columns // tile,),
        out_shape=(
            jax.ShapeDtypeStruct(weight.shape, weight.dtype),
            jax.ShapeDtypeStruct((8, columns), F32),
        ),
        in_specs=in_specs,
        out_specs=(block, pl.BlockSpec((8, tile), lambda i: (0, i))),
        input_output_aliases={} if buf is None else {3: 0},
        compiler_params=pltpu.CompilerParams(vmem_limit_bytes=grant),
        cost_estimate=pl.CostEstimate(
            flops=2 * depth * tokens * columns, bytes_accessed=4 * depth * columns, transcendentals=0
        ),
    )(*args)


def body(n_latent, n_rows, activations_in, gate_proj, up_proj, down_proj, enc_weight, enc_bias, dec_weight, dec_bias):
    tokens = activations_in.shape[1]
    width, local = enc_weight.shape
    here = activations_in.reshape(tokens, activations_in.shape[2])
    if n_latent == n_rows:
        pairs = [(a * n_rows + b, b * n_rows + a) for a in range(n_latent) for b in range(n_rows)]
        portion = lax.ppermute(here, ("latent", "rows"), pairs)
    else:
        everything = lax.all_gather(here, "latent", axis=1, tiled=True)
        portion = lax.dynamic_slice_in_dim(everything, lax.axis_index("rows") * width, width, 1)
    if n_latent <= 8:
        scatter_l = lambda v, wire: direct_scatter(v, "latent", n_latent, wire)
        gather_l = lambda v: direct_gather(v, "latent", n_latent)
    else:
        scatter_l = lambda v, wire: lax.psum_scatter(v, "latent", scatter_dimension=0, tiled=True)
        gather_l = lambda v: lax.all_gather(v, "latent", axis=0, tiled=True)

    gate_part = jnp.dot(portion, gate_proj, preferred_element_type=F32)
    up_part = jnp.dot(portion, up_proj, preferred_element_type=F32)
    both = jnp.concatenate([gate_part, up_part], axis=1).astype(BF16)
    both = halves_scatter(both, "rows", n_rows, BF16)
    gate_term, up_term = both[:, :gate_proj.shape[1]], both[:, gate_proj.shape[1]:]
    hidden = (jax.nn.gelu(gate_term, approximate=True) * up_term).astype(BF16)
    hidden = halves_gather(hidden, "rows", n_rows)
    partial_value = lax.dot_general(down_proj, hidden, (((0,), (1,)), ((), ())), preferred_element_type=F32)
    inputs_here = scatter_l(partial_value, BF16).astype(BF16)
    inputs = gather_l(inputs_here)
    share = inputs_here.shape[0]
    bias_here = lax.dynamic_slice_in_dim(dec_bias, lax.axis_index("latent") * share, share, 0)

    enc_scale = MODEL_WIDTH ** (-0.5)
    dec_scale = LATENTS ** (-0.5)
    dec_turned = dec_weight.T
    chunks = max(1, min(4, local // 512))
    step = local // chunks
    spans = [slice(c * step, (c + 1) * step) for c in range(chunks)]
    over_width = (((0,), (0,)), ((), ()))
    local_rebuilt = jnp.zeros((width, tokens), F32)
    latents, pres = [], []
    for span in spans:
        part = lax.dot_general(inputs, enc_weight[:, span], over_width, preferred_element_type=F32).astype(BF16)
        encoded = halves_scatter(part, "rows", n_rows, BF16)
        pre = enc_scale * encoded + enc_bias[span]
        pres.append(pre)
        mine = (jax.nn.softplus(sharpness * pre) / sharpness).astype(BF16)
        full = halves_gather(mine, "rows", n_rows)
        latents.append(full)
        local_rebuilt = local_rebuilt + lax.dot_general(
            dec_turned[:, span], full, (((1,), (1,)), ((), ())), preferred_element_type=F32
        )
    rebuilt_share = scatter_l(local_rebuilt, F32)
    grad_share = (
        2.0 * (dec_scale * rebuilt_share + bias_here[:, None] - inputs_here.astype(F32))
    ).astype(BF16)
    residual_grad = gather_l(grad_share)
    grads = []
    for c, span in enumerate(spans):
        part = lax.dot_general(residual_grad, dec_turned[:, span], over_width, preferred_element_type=F32).astype(BF16)
        back = halves_scatter(part, "rows", n_rows, BF16)
        mine = (jax.nn.sigmoid(sharpness * pres[c]) * (dec_scale * back + sparsity_cost)).astype(BF16)
        grads.append(halves_gather(mine, "rows", n_rows))
    dec_new = enc_new = None
    for c, span in enumerate(spans):
        dec_new, _ = update(weight_rate * dec_scale, residual_grad, latents[c], dec_turned, c * step, dec_new, 24 << 20)
    sums = []
    for c, span in enumerate(spans):
        enc_new, total = update(weight_rate * enc_scale, inputs, grads[c], enc_weight, c * step, enc_new, 52 << 20)
        sums.append(total[0])
    enc_bias = enc_bias - enc_bias_rate * jnp.concatenate(sums)
    dec_bias = dec_bias - dec_bias_rate * jnp.sum(residual_grad, axis=1, dtype=F32)
    return (enc_new, enc_bias, dec_new.T, dec_bias)


MESH = pl.DeviceIdType.MESH
HALVES = 2
LEAD = 3
RING = 4
STAGED = 4


def softplus(v):
    return jnp.maximum(v, 0.0) + jnp.log1p(jnp.exp(-jnp.abs(v)))


def over_last(a, b):
    return lax.dot_general(a, b, (((1,), (1,)), ((), ())), preferred_element_type=F32)


def train_kernel(
    n_latent, n_rows, chunk,
    act_ref, gate_ref, up_ref, down_ref, enc_ref, bias_ref, dec_ref, dec_bias_ref,
    enc, dec, grads, features, resid,
    act_turned, act_own, act, gate_up, down,
    ffn_part, ffn_got, ffn_sum, ffn_far, hidden,
    acc, value, value_got, share, resid_got, resid_share, resid_turned,
    part, pair, far_got, latents,
    load_sem, weight_sem, act_send, act_sem, ffn_send, ffn_sem, z_send, z_sem,
    part_send, part_sem, pair_send, pair_sem, full_send, full_sem,
):
    rows = lax.axis_index("rows")
    z = lax.axis_index("latent")
    core = lax.rem(rows, 2)
    mate = {"rows": rows + 1 - 2 * core}
    far = {"rows": lax.rem(rows + 2, n_rows)}
    others = [{"latent": lax.rem(z + s, n_latent)} for s in range(1, n_latent)]
    half = act.shape[1]
    own = half // 2
    small = half // n_latent
    width, local_hidden = gate_ref.shape
    count = enc.shape[0]
    items = HALVES * count
    mine = pl.ds(pl.multiple_of(core * own, own), own)
    theirs = pl.ds(pl.multiple_of((1 - core) * own, own), own)
    small_of = lambda at: pl.ds(pl.multiple_of(at * small, small), small)
    my_small = small_of(z)

    def remote(src, dst, send, recv, to):
        return pltpu.make_async_remote_copy(
            src_ref=src, dst_ref=dst, send_sem=send, recv_sem=recv, device_id=to, device_id_type=MESH
        )

    loads = [
        pltpu.make_async_copy(act_ref, act_turned, load_sem.at[0]),
        pltpu.make_async_copy(gate_ref, gate_up.at[:, :local_hidden], load_sem.at[1]),
        pltpu.make_async_copy(up_ref, gate_up.at[:, local_hidden:], load_sem.at[2]),
        pltpu.make_async_copy(down_ref, down, load_sem.at[3]),
    ]
    for load in loads:
        load.start()
    weights = []
    for c in range(count):
        span = slice(c * chunk, (c + 1) * chunk)
        weights.append(pltpu.make_async_copy(enc_ref.at[:, span], enc.at[c], weight_sem.at[0, c]))
        weights.append(pltpu.make_async_copy(dec_ref.at[:, span], dec.at[c], weight_sem.at[1, c]))

    barrier = pltpu.get_barrier_semaphore()
    for to in [mate, far] + others:
        pl.semaphore_signal(barrier, inc=1, device_id=to, device_id_type=MESH)
    loads[0].wait()
    turned = act_turned[...].T
    for h in range(HALVES):
        act_own[h] = turned[h * half:(h + 1) * half]
    pl.semaphore_wait(barrier, n_latent + 1)

    def act_copy(h, s):
        return remote(act_own.at[h], act.at[h], act_send.at[h, s], act_sem.at[h], others[s])

    @pl.when(z == rows)
    def _():
        for h in range(HALVES):
            for s in reversed(range(n_latent - 1)):
                act_copy(h, s).start()
        for h in range(HALVES):
            act[h] = act_own[h]

    for load in loads[1:]:
        load.wait()
    for load in weights:
        load.start()

    @pl.when(z != rows)
    def _():
        act_copy(0, 0).wait_recv()


    def ffn_copy(stage, h):
        src, dst, to = (
            (ffn_part.at[h, theirs], ffn_got.at[h], mate),
            (ffn_sum.at[h], ffn_far.at[h], far),
            (hidden.at[h, mine], hidden.at[h, mine], mate),
        )[stage]
        return remote(src, dst, ffn_send.at[stage, h], ffn_sem.at[stage, h], to)

    def z_copies(stage, h):
        copies = []
        for s in range(n_latent - 1):
            to = lax.rem(z + s + 1, n_latent)
            src, dst = (
                (value.at[h, small_of(to)], value_got.at[h, s]),
                (share.at[h], features.at[h, my_small]),
                (acc.at[h, small_of(to)], resid_got.at[h, s]),
                (resid_share.at[h], resid.at[h, my_small]),
            )[stage]
            copies.append(remote(src, dst, z_send.at[stage, h, s], z_sem.at[stage, h, s], others[s]))
        return copies

    for h in range(HALVES):
        if h > 0:
            @pl.when(z != rows)
            def _():
                act_copy(h, 0).wait_recv()
        ffn_part[h] = jnp.dot(act[h], gate_up[...], preferred_element_type=F32).astype(BF16)
        ffn_copy(0, h).start()
        ffn_copy(0, h).wait_recv()
        ffn_sum[h] = (ffn_part[h, mine].astype(F32) + ffn_got[h].astype(F32)).astype(BF16)
        ffn_copy(1, h).start()
    for h in range(HALVES):
        ffn_copy(1, h).wait_recv()
        total = ffn_sum[h].astype(F32) + ffn_far[h].astype(F32)
        gate_term, up_term = total[:, :local_hidden], total[:, local_hidden:]
        hidden[h, mine] = (jax.nn.gelu(gate_term, approximate=True) * up_term).astype(BF16)
        ffn_copy(2, h).start()
        ffn_copy(2, h).wait_recv()
        part_value = over_last(hidden[h], down[...])
        acc[h] = part_value
        value[h] = part_value.astype(BF16)
        for copy in z_copies(0, h):
            copy.start()
    for h in range(HALVES):
        total = acc[h, my_small]
        for s, copy in enumerate(z_copies(0, h)):
            copy.wait_recv()
            total = total + value_got[h, s].astype(F32)
        share[h] = total.astype(BF16)
        features[h, my_small] = total.astype(BF16)
        for copy in z_copies(1, h):
            copy.start()
        acc[h] = jnp.zeros_like(acc[h])
    for load in weights:
        load.wait()
    for copy in z_copies(1, 0):
        copy.wait_recv()

    enc_scale = MODEL_WIDTH ** (-0.5)
    dec_scale = LATENTS ** (-0.5)

    def near_copy(i):
        slot = lax.rem(i, RING)
        return remote(part.at[slot, theirs], grads.at[lax.rem(i, items), theirs], part_send.at[slot], part_sem.at[i], mate)

    def far_copy(i):
        return remote(pair.at[i], far_got.at[i], pair_send.at[i], pair_sem.at[i], far)

    def full_copy(i, full, j):
        return remote(full.at[j, mine], full.at[j, mine], full_send.at[i], full_sem.at[i], mate)

    def dot_step(i, phase, reuse):
        j = i - phase * items
        h, c = j // count, lax.rem(j, count)
        if reuse:
            near_copy(i - RING).wait_send()
        left, right = ((features, enc), (resid, dec))[phase]
        slot = lax.rem(i, RING)
        part[slot] = jnp.dot(left[h], right[c], preferred_element_type=F32).astype(BF16)
        near_copy(i).start()

    def pair_step(i):
        near_copy(i).wait_recv()
        slot = lax.rem(i, RING)
        pair[i] = (part[slot, mine].astype(F32) + grads[lax.rem(i, items), mine].astype(F32)).astype(BF16)
        far_copy(i).start()

    def pre_of(j):
        return enc_scale * (pair[j].astype(F32) + far_got[j].astype(F32)) + bias_ref[lax.rem(j, count)]

    def full_step(i, phase):
        j = i - phase * items
        far_copy(i).wait_recv()
        if phase == 0:
            latents[j, mine] = (softplus(sharpness * pre_of(j)) / sharpness).astype(BF16)
            full_copy(i, latents, j).start()
        else:
            back = pair[i].astype(F32) + far_got[i].astype(F32)
            slope = jax.nn.sigmoid(sharpness * pre_of(j))
            grads[j, mine] = (slope * (dec_scale * back + sparsity_cost)).astype(BF16)
            full_copy(i, grads, j).start()

    def use_step(i, phase):
        j = i - phase * items
        full = (latents, grads)[phase]
        full_copy(i, full, j).wait_recv()
        if phase == 0:
            h, c = j // count, lax.rem(j, count)
            acc[h] += over_last(full[j], dec[c])

    def turn_resid():
        resid_turned[...] = jnp.concatenate([resid[h] for h in range(HALVES)], axis=0).T

    def dec_step(c):
        def tile_step(t, carry):
            span = pl.ds(pl.multiple_of(t * TILE, TILE), TILE)
            right = jnp.concatenate([latents[h * count + c, :, span] for h in range(HALVES)], axis=0)
            grad = jnp.dot(resid_turned[...], right, preferred_element_type=F32)
            dec[c, :, span] = (dec[c, :, span].astype(F32) - weight_rate * dec_scale * grad).astype(BF16)
            return carry

        lax.fori_loop(0, chunk // TILE, tile_step, 0)

    last_dots = 2 * items - count - LEAD + 1

    def run(first, last):
        if last <= first:
            return

        def body(i, carry):
            if first + LEAD < 2 * items:
                dot_step(i + LEAD, (first + LEAD) // items, True)
            if first + LEAD - 1 < 2 * items:
                pair_step(i + LEAD - 1)
            full_step(i, first // items)
            use_step(i - 1, (first - 1) // items)
            if last_dots <= first < last_dots + count:
                dec_step(i - last_dots)
            return carry

        lax.fori_loop(first, last, body, 0)

    def resid_step(h):
        total = acc[h, my_small]
        for s, copy in enumerate(z_copies(2, h)):
            copy.wait_recv()
            total = total + resid_got[h, s]
        grad = 2.0 * (dec_scale * total + dec_bias_ref[...].reshape(1, width) - share[h].astype(F32))
        resid_share[h] = grad.astype(BF16)
        resid[h, my_small] = grad.astype(BF16)
        for copy in z_copies(3, h):
            copy.start()

    for i in range(LEAD):
        dot_step(i, 0, False)
    for i in range(LEAD - 1):
        pair_step(i)
    dot_step(LEAD, 0, LEAD >= RING)
    pair_step(LEAD - 1)
    full_step(0, 0)
    marks = {}
    for h in range(HALVES):
        marks.setdefault((h + 1) * count + 1, []).append(lambda h=h: [copy.start() for copy in z_copies(2, h)])
        marks.setdefault((h + 1) * count + 3, []).append(lambda h=h: resid_step(h))
        marks.setdefault(items + h * count - LEAD, []).append(
            lambda h=h: [copy.wait_recv() for copy in z_copies(3, h)]
        )
        if h > 0:
            marks.setdefault(h * count - LEAD, []).append(lambda h=h: [copy.wait_recv() for copy in z_copies(1, h)])
    marks.setdefault(last_dots, []).append(turn_resid)
    cuts = set(marks) | {1, items - LEAD, items - LEAD + 1, items, items + 1}
    cuts |= {2 * items - LEAD, 2 * items - LEAD + 1, last_dots + count, 2 * items}
    cuts = sorted(cuts)
    for first, last in zip(cuts[:-1], cuts[1:]):
        for act_on in marks.get(first, []):
            act_on()
        run(first, last)
    use_step(2 * items - 1, 1)

    @pl.when(z == rows)
    def _():
        for h in range(HALVES):
            for s in range(n_latent - 1):
                act_copy(h, s).wait_send()

    for h in range(HALVES):
        for stage in range(3):
            ffn_copy(stage, h).wait_send()
        for stage in range(4):
            for copy in z_copies(stage, h):
                copy.wait_send()
    for i in range(2 * items - RING, 2 * items):
        near_copy(i).wait_send()

    def drain(i, carry):
        for phase, full in ((0, latents), (1, grads)):
            at = i + phase * items
            far_copy(at).wait_send()
            full_copy(at, full, i).wait_send()
        return carry

    lax.fori_loop(0, items, drain, 0)


def write_kernel(
    enc, dec, grads, features, resid, bias_ref, dec_bias_ref, enc_out, dec_out, bias_out, dec_bias_out,
    turned, staged, enc_sem, dec_sem,
):
    count, _, chunk = enc.shape
    enc_rate = weight_rate * MODEL_WIDTH ** (-0.5)

    def out_copies(c):
        span = slice(c * chunk, (c + 1) * chunk)
        return (
            pltpu.make_async_copy(dec.at[c], dec_out.at[:, span], dec_sem.at[c]),
            pltpu.make_async_copy(staged.at[c % STAGED], enc_out.at[:, span], enc_sem.at[c]),
        )

    copies = [out_copies(c) for c in range(count)]
    turned[...] = jnp.concatenate([features[h] for h in range(HALVES)], axis=0).T
    for c in range(count):
        copies[c][0].start()
        if c >= STAGED:
            copies[c - STAGED][1].wait()

        def tile_step(t, carry):
            span = pl.ds(pl.multiple_of(t * WIDE, WIDE), WIDE)
            right = jnp.concatenate([grads[h * count + c, :, span] for h in range(HALVES)], axis=0)
            grad = jnp.dot(turned[...], right, preferred_element_type=F32)
            staged[c % STAGED, :, span] = (enc[c, :, span].astype(F32) - enc_rate * grad).astype(BF16)
            total = jnp.sum(right.astype(F32), axis=0, keepdims=True)
            bias_out[c, :, span] = bias_ref[c, :, span] - enc_bias_rate * total
            return carry

        lax.fori_loop(0, chunk // WIDE, tile_step, 0)
        copies[c][1].start()
    total = sum(jnp.sum(resid[h].astype(F32), axis=0) for h in range(HALVES))
    dec_bias_out[...] = dec_bias_ref[...] - dec_bias_rate * total
    for c in range(count):
        copies[c][0].wait()
        if c >= count - STAGED:
            copies[c][1].wait()


def fast_body(n_latent, n_rows, activations_in, gate_proj, up_proj, down_proj, enc_weight, enc_bias, dec_weight, dec_bias):
    tokens = activations_in.shape[1]
    width, local = enc_weight.shape
    hidden = gate_proj.shape[1]
    chunk = local // CHUNKS
    half = tokens // HALVES
    own, small, items = half // 2, half // n_latent, HALVES * CHUNKS
    dec_turned = dec_weight.T
    any_spec = pl.BlockSpec(memory_space=pl.ANY)
    vmem_spec = pl.BlockSpec(memory_space=pltpu.VMEM)
    vmem, dma = pltpu.VMEM, pltpu.SemaphoreType.DMA
    between = n_latent - 1
    enc_held, dec_held, grads, inputs, residual_grad = pl.pallas_call(
        functools.partial(train_kernel, n_latent, n_rows, chunk),
        out_shape=(
            vmem((CHUNKS, width, chunk), BF16),
            vmem((CHUNKS, width, chunk), BF16),
            vmem((items, half, chunk), BF16),
            vmem((HALVES, half, width), BF16),
            vmem((HALVES, half, width), BF16),
        ),
        in_specs=[any_spec] * 5 + [vmem_spec, any_spec, vmem_spec],
        out_specs=(vmem_spec,) * 5,
        scratch_shapes=[
            vmem((width, tokens), BF16),
            vmem((HALVES, half, width), BF16),
            vmem((HALVES, half, width), BF16),
            vmem((width, 2 * hidden), BF16),
            vmem((width, hidden), BF16),
            vmem((HALVES, half, 2 * hidden), BF16),
            vmem((HALVES, own, 2 * hidden), BF16),
            vmem((HALVES, own, 2 * hidden), BF16),
            vmem((HALVES, own, 2 * hidden), BF16),
            vmem((HALVES, half, hidden), BF16),
            vmem((HALVES, half, width), F32),
            vmem((HALVES, half, width), BF16),
            vmem((HALVES, between, small, width), BF16),
            vmem((HALVES, small, width), BF16),
            vmem((HALVES, between, small, width), F32),
            vmem((HALVES, small, width), BF16),
            vmem((width, tokens), BF16),
            vmem((RING, half, chunk), BF16),
            vmem((2 * items, own, chunk), BF16),
            vmem((2 * items, own, chunk), BF16),
            vmem((items, half, chunk), BF16),
            dma((4,)),
            dma((2, CHUNKS)),
            dma((HALVES, between)),
            dma((HALVES,)),
            dma((3, HALVES)),
            dma((3, HALVES)),
            dma((4, HALVES, between)),
            dma((4, HALVES, between)),
            dma((RING,)),
            dma((2 * items,)),
            dma((2 * items,)),
            dma((2 * items,)),
            dma((2 * items,)),
            dma((2 * items,)),
        ],
        compiler_params=pltpu.CompilerParams(collective_id=0, has_side_effects=True, vmem_limit_bytes=GRANT),
    )(
        activations_in.reshape(tokens, activations_in.shape[2]).T, gate_proj, up_proj, down_proj.T, enc_weight,
        enc_bias.reshape(CHUNKS, 1, chunk), dec_turned, dec_bias,
    )
    enc_held, dec_held, grads, inputs, residual_grad = (
        pltpu.with_memory_space_constraint(v, vmem) for v in (enc_held, dec_held, grads, inputs, residual_grad)
    )
    enc_new, dec_new, enc_bias, dec_bias = pl.pallas_call(
        write_kernel,
        out_shape=(
            jax.ShapeDtypeStruct((width, local), BF16),
            jax.ShapeDtypeStruct((width, local), BF16),
            jax.ShapeDtypeStruct((CHUNKS, 1, chunk), F32),
            jax.ShapeDtypeStruct((width,), F32),
        ),
        in_specs=[vmem_spec] * 7,
        out_specs=(any_spec, any_spec, vmem_spec, vmem_spec),
        scratch_shapes=[
            vmem((width, tokens), BF16),
            vmem((STAGED, width, chunk), BF16),
            dma((CHUNKS,)),
            dma((CHUNKS,)),
        ],
        compiler_params=pltpu.CompilerParams(vmem_limit_bytes=GRANT),
    )(enc_held, dec_held, grads, inputs, residual_grad, enc_bias.reshape(CHUNKS, 1, chunk), dec_bias)
    return (enc_new, enc_bias.reshape(local), dec_new.T, dec_bias)


def solution(mesh):
    def step(*args):
        return run(mesh.shape["latent"], mesh.shape["rows"], *args)

    small = mesh.shape["latent"] == mesh.shape["rows"] == 4
    run = fast_body if small else body


    return jax.shard_map(
        step,
        mesh=mesh,
        in_specs=(
            P("groups", None, "latent"),
            P("rows", "latent"),
            P("rows", "latent"),
            P("latent", "rows"),
            P(("groups", "rows"), "latent"),
            P(("groups", "latent")),
            P(("groups", "latent"), "rows"),
            P(("groups", "rows")),
        ),
        out_specs=(
            P(("groups", "rows"), "latent"),
            P(("groups", "latent")),
            P(("groups", "latent"), "rows"),
            P(("groups", "rows")),
        ),
        check_vma=False,
    )
```
